512 devices in a mesh: gz: 4 (over y), gy: 4 (over x_lo, core), col: 32 (over z, x_hi).
Axes of the slice: x: 4 (x_hi: 2, x_lo: 2; x = x_hi * 2 + x_lo), y: 4, z: 16, core: 2. Of those that a mesh axis runs over, the one named last changes fastest.
Arguments:
- volume: bfloat16 [8, 8, 1024, 128], P('gz', 'gy', 'col'), may hold values from -6 to 6
- conv_weight: bfloat16 [27, 2, 1024, 1024], P(None, None, 'col'), may hold values from -0.0390625 to 0.0390625
- proj_weight: bfloat16 [1024, 512], replicated, may hold values from -0.1875 to 0.1875
Outputs:
- fine_tiles: float32 [32, 32, 4096], P('gz', 'gy', 'col')
The draws below stay inside these ranges and needn't reach their ends.
All inputs are finite; a program needn't handle non-finite values.
Results may differ from the reference program's by a relative error of at most 0.0029.
Values may be sent and summed in bfloat16 or wider, within the bound.
No kernel may reach another device: no remote copies, remote signals or barrier semaphores. Data moves between devices by JAX's collectives and lax.ppermute only.
A program may use at most 64 MiB of HBM per device.

```python
import jax
import jax.numpy as jnp
from jax import lax

C = 1024
CO = 1024
F = 32
P_SIZE = 512
BX = 128
NZ = 8
NY = 8


def block_levels(own_key, extent, split, least, high):
    loudness, own = 1.0, jax.random.fold_in(own_key, 6)
    for dim, blocks in split:
        draws = jnp.exp(jax.random.uniform(jax.random.fold_in(own, dim), (blocks,), jnp.float32, least / len(split), high / len(split)))
        loudness = loudness * jnp.repeat(draws, extent[dim] // blocks).reshape([-1 if axis == dim else 1 for axis in range(len(extent))])
    return loudness


def centred(own_key, dims, scale, limit, pieces=(), kind=jnp.bfloat16):
    gain = block_levels(own_key, dims, pieces, -0.22, 0.18) if pieces else 1.0
    values = jax.random.normal(own_key, dims, jnp.float32) * scale * gain
    return jnp.minimum(jnp.maximum(values, -limit), limit).astype(kind)


def setup_inputs(seed: int = 0) -> dict:
    splits = jax.random.split(jax.random.key(seed), 4)
    volume = centred(splits[0], (NZ, NY, C, BX), 1.0, 6.0, ((0, 4), (1, 4), (2, 32)))
    conv_weight = centred(splits[1], (27, 2, CO, C), (27 * C) ** -0.5, 0.0390625, ((2, 32),))
    proj_weight = centred(splits[2], (CO, P_SIZE), CO ** -0.5, 0.1875)
    return dict(volume=volume, conv_weight=conv_weight, proj_weight=proj_weight)


def inverse_lift(low_band, high_band, along):
    length = low_band.shape[along]

    def window_of(array, first, last):
        return lax.slice_in_dim(array, first, last, axis=along)

    even_rows = window_of(low_band, 1, length - 1) - 0.25 * (window_of(high_band, 0, length - 2) + window_of(high_band, 1, length - 1))
    next_even = window_of(low_band, 2, length) - 0.25 * (window_of(high_band, 1, length - 1) + window_of(high_band, 2, length))
    odd_rows = window_of(high_band, 1, length - 1) + 0.5 * (even_rows + next_even)
    paired = jnp.stack([even_rows, odd_rows], axis=along + 1)
    new_shape = list(even_rows.shape)
    new_shape[along] = 2 * (length - 2)
    return paired.reshape(new_shape)


def synthesize(coefficients):
    quarter = coefficients.shape[-1] // 4
    bands = coefficients.reshape(coefficients.shape[:-1] + (4, quarter))
    low_z = inverse_lift(bands[..., 0, :], bands[..., 2, :], 0)
    high_z = inverse_lift(bands[..., 1, :], bands[..., 3, :], 0)
    return inverse_lift(low_z, high_z, 1)


def reference(volume, conv_weight, proj_weight):
    kernel = conv_weight.astype(jnp.float32).reshape((3, 3, 3, 2 * CO, C))
    conv_out = lax.conv_general_dilated(volume.astype(jnp.float32)[None], kernel, (1, 1, 1), ((1, 1), (1, 1), (1, 1)), dimension_numbers=("NDHCW", "DHWOI", "NDHCW"), precision=lax.Precision.HIGHEST)[0]
    gate_half = conv_out[:, :, :CO, :]
    values_half = conv_out[:, :, CO:, :]
    gated_values = (jax.nn.silu(gate_half) * values_half).astype(jnp.bfloat16)
    coefficients = jnp.einsum("zycx,cp->zyxp", gated_values.astype(jnp.float32), proj_weight.astype(jnp.float32), precision=lax.Precision.HIGHEST)
    padded = jnp.pad(coefficients, ((1, 1), (1, 1), (0, 0), (0, 0)), mode="wrap")
    middle = synthesize(padded)
    padded_middle = jnp.pad(middle, ((1, 1), (1, 1), (0, 0), (0, 0)), mode="wrap")
    fine_tiles = synthesize(padded_middle)
    return fine_tiles.reshape((4 * NZ, 4 * NY, BX * F))
```

```python
import jax
import jax.numpy as jnp
from jax import lax
from jax.experimental import pallas as pl
from jax.experimental.pallas import tpu as pltpu
from jax.sharding import Mesh, PartitionSpec as P

F32 = jnp.float32
BF16 = jnp.bfloat16
VMEM = pl.BlockSpec(memory_space=pltpu.VMEM)
SMEM = pl.BlockSpec(memory_space=pltpu.SMEM)


def conv_kernel(half_ref, own_ref, other_ref, weight_ref, low_ref, inner_ref, high_ref, cells, total):
    step = pl.program_id(0)

    @pl.when(step == 0)
    def _():
        half = half_ref[0]
        for k in range(16):
            for row in range(4):
                lanes = pl.ds(row * 128, 128)
                cells[k, half, :, lanes] = own_ref[k, row]
                cells[k, 1 - half, :, lanes] = other_ref[k, row]
        total[...] = jnp.zeros_like(total)

    products = jnp.dot(
        weight_ref[0], cells[...].reshape(1024, 512), preferred_element_type=F32
    )
    lane = lax.broadcasted_iota(jnp.int32, (64, 128), 1)
    for dy in range(3):
        for z in range(2):
            for y in range(2):
                row = z * 2 + y
                before, centre, after = (
                    products[(dy * 3 + dx) * 64 : (dy * 3 + dx + 1) * 64, row * 128 : (row + 1) * 128]
                    for dx in range(3)
                )
                term = (
                    centre
                    + jnp.where(lane == 0, 0.0, pltpu.roll(before, 1, 1))
                    + jnp.where(lane == 127, 0.0, pltpu.roll(after, 127, 1))
                )
                total[z + 2 - step, y + 2 - dy] += term

    @pl.when(step == 2)
    def _():
        for z in range(4):
            low_ref[z] = total[z, 0]
            inner_ref[z, 0] = total[z, 1]
            inner_ref[z, 1] = total[z, 2]
            high_ref[z] = total[z, 3]


def convolve(half, own, other, weight):
    whole = lambda shape: pl.BlockSpec(shape, lambda i: (0,) * len(shape))
    return pl.pallas_call(
        conv_kernel,
        grid=(3,),
        in_specs=[
            SMEM,
            whole((16, 4, 32, 128)),
            whole((16, 4, 32, 128)),
            pl.BlockSpec((1, 576, 1024), lambda i: (i, 0, 0)),
        ],
        out_specs=[whole((4, 64, 128)), whole((4, 2, 64, 128)), whole((4, 64, 128))],
        out_shape=[
            jax.ShapeDtypeStruct((4, 64, 128), F32),
            jax.ShapeDtypeStruct((4, 2, 64, 128), F32),
            jax.ShapeDtypeStruct((4, 64, 128), F32),
        ],
        scratch_shapes=[pltpu.VMEM((16, 2, 32, 512), BF16), pltpu.VMEM((4, 4, 64, 128), F32)],
        name="conv",
    )(half, own, other, weight)


def edge_kernel(inner_ref, before_ref, after_ref, low_ref, high_ref):
    for ref, z in ((low_ref, 0), (high_ref, 3)):
        ref[0] = inner_ref[z, 0] + before_ref[z]
        ref[1] = inner_ref[z, 1] + after_ref[z]


def edges(inner, before, after):
    shape = jax.ShapeDtypeStruct((2, 64, 128), F32)
    return pl.pallas_call(
        edge_kernel, in_specs=[VMEM] * 3, out_specs=[VMEM] * 2, out_shape=[shape, shape], name="edges"
    )(inner, before, after)


def gate_kernel(slot_ref, inner_ref, before_ref, after_ref, under_ref, over_ref, out_ref, turned, packed):
    slot = slot_ref[0]
    group = lax.broadcasted_iota(jnp.int32, (128, 128), 0) // 32
    for z in range(2):
        for y in range(2):
            side = (before_ref, after_ref)[y]
            ends = (under_ref, over_ref)[z]
            conv_out = inner_ref[z + 1, y] + side[z + 1] + ends[y]
            gate, value = conv_out[:32], conv_out[32:]
            gated = gate / (1.0 + jnp.exp(-gate)) * value
            spread = jnp.where(group == slot, jnp.concatenate([gated] * 4, axis=0), 0.0)
            turned[...] = spread.T
            for i in range(4):
                packed[pl.ds(i * 4 + z * 2 + y, 32, stride=16), :] = turned[pl.ds(i, 32, stride=4), :]
    out_ref[...] = packed[...].reshape(32, 16, 128).astype(BF16)


def gate(slot, inner, before, after, under, over):
    return pl.pallas_call(
        gate_kernel,
        in_specs=[SMEM] + [VMEM] * 5,
        out_specs=VMEM,
        out_shape=jax.ShapeDtypeStruct((32, 16, 128), BF16),
        scratch_shapes=[pltpu.VMEM((128, 128), F32), pltpu.VMEM((512, 128), F32)],
        name="gate",
    )(slot, inner, before, after, under, over)


def project_kernel(parts_ref, proj_ref, out_ref, held):
    chunks = []
    for k in range(8):
        chunk = parts_ref[4 * k].astype(F32)
        for i in range(1, 4):
            chunk = chunk + parts_ref[4 * k + i].astype(F32)
        chunks.append(chunk.astype(BF16))
    held[...] = jnp.dot(
        jnp.concatenate(chunks, axis=1), proj_ref[...], preferred_element_type=F32
    )
    block = lax.broadcasted_iota(jnp.int32, (4, 128), 1) // 32
    for b1 in range(4):
        rows = [held[i * 4 : (i + 1) * 4, b1 * 128 : (b1 + 1) * 128] for i in range(4)]
        hz1, hy1 = b1 // 2, b1 % 2
        for b2 in range(4):
            hz2, hy2 = b2 // 2, b2 % 2
            merged = None
            for i in range(4):
                shift = ((i - b2) % 4) * 32
                moved = rows[i] if shift == 0 else pltpu.roll(rows[i], shift, 1)
                merged = moved if merged is None else jnp.where(block == i, moved, merged)
            for z in range(2):
                for y in range(2):
                    at = ((z * 2 + hz1) * 2 + hz2) * 8 + y * 4 + hy1 * 2 + hy2
                    out_ref[at : at + 1, :] = merged[z * 2 + y : z * 2 + y + 1, :]


def project(parts, proj_weight):
    return pl.pallas_call(
        project_kernel,
        in_specs=[VMEM] * 2,
        out_specs=VMEM,
        out_shape=jax.ShapeDtypeStruct((64, 128), F32),
        scratch_shapes=[pltpu.VMEM((16, 512), F32)],
        name="project",
    )(parts, proj_weight)


def lift_pair(low, high):
    n = len(low)
    even = [low[i] - 0.25 * (high[i - 1] + high[i]) for i in range(1, n)]
    odd = [high[i] + 0.5 * (even[i - 1] + even[i]) for i in range(1, n - 1)]
    result = []
    for i in range(n - 2):
        result += [even[i], odd[i]]
    return result + [even[n - 2]]


def two_levels(cells):
    middle = [lift_pair([c[0][b] for c in cells], [c[1][b] for c in cells])[1:] for b in range(2)]
    return lift_pair(middle[0], middle[1])[:8]


def rows_of(ref, cell):
    return [[ref[pl.ds(((cell * 2 + h1) * 2 + h2) * 8, 8), :] for h2 in range(2)] for h1 in range(2)]


def extended_rows(own_ref, before_ref, after_ref):
    return [
        rows_of(before_ref, 0),
        rows_of(before_ref, 1),
        rows_of(own_ref, 0),
        rows_of(own_ref, 1),
        rows_of(after_ref, 0),
    ]


def lift_kernel(own_ref, before_ref, after_ref, out_ref):
    for i, fine in enumerate(two_levels(extended_rows(own_ref, before_ref, after_ref))):
        out_ref[pl.ds(i, 8, stride=8), :] = fine


def lift(own, before, after):
    return pl.pallas_call(
        lift_kernel,
        in_specs=[VMEM] * 3,
        out_specs=VMEM,
        out_shape=jax.ShapeDtypeStruct((64, 128), F32),
        name="lift",
    )(own, before, after)


def from_neighbours(to_next, to_previous, axis, closed):
    count = lax.axis_size(axis)
    ends = count if closed else count - 1
    before = lax.ppermute(to_next, axis, [(i, (i + 1) % count) for i in range(ends)])
    after = lax.ppermute(to_previous, axis, [((i + 1) % count, i) for i in range(ends)])
    return before, after


def on_device(volume, conv_weight, proj_weight):
    half = lax.axis_index("half")
    slot = (lax.axis_index("ring") * 2 + half) % 4
    own = lax.all_gather(volume.reshape(4, 32, 128), "ring", axis=0, tiled=False)
    other = lax.ppermute(own, "half", [(0, 1), (1, 0)])
    low, inner, high = convolve(
        half.reshape(1), own, other, conv_weight.reshape(3, 576, 1024)
    )
    before, after = from_neighbours(high, low, "gy", False)
    bottom, top = edges(inner, before, after)
    under, over = from_neighbours(top, bottom, "gz", False)
    sent = gate(slot.reshape(1), inner, before, after, under, over)
    parts = lax.all_to_all(sent, ("ring", "half"), split_axis=0, concat_axis=0, tiled=True)
    coefficients = project(parts, proj_weight)
    tall = lift(coefficients, *from_neighbours(coefficients, coefficients, "gz", True))
    fine = lift(tall, *from_neighbours(tall, tall, "gy", True))
    return fine.reshape(8, 8, 128)


def solution(mesh):
    split = Mesh(mesh.devices.reshape(4, 4, 16, 2), ("gz", "gy", "ring", "half"))
    col = ("ring", "half")
    return jax.shard_map(
        on_device,
        mesh=split,
        in_specs=(P("gz", "gy", col, None), P(None, None, col, None), P()),
        out_specs=P("gz", "gy", col),
        check_vma=False,
    )
```

```python
import jax
import jax.numpy as jnp
from jax import lax
from jax.experimental import pallas as pl
from jax.experimental.pallas import tpu as pltpu
from jax.sharding import Mesh, PartitionSpec as P

F32 = jnp.float32
BF16 = jnp.bfloat16
VMEM = pl.BlockSpec(memory_space=pltpu.VMEM)
SMEM = pl.BlockSpec(memory_space=pltpu.SMEM)


def conv_kernel(half_ref, own_ref, other_ref, weight_ref, keep_ref, y_ref, z_ref, corner_ref, cells, total):
    step = pl.program_id(0)

    @pl.when(step == 0)
    def _():
        half = half_ref[0]
        for k in range(16):
            for row in range(4):
                lanes = pl.ds(row * 128, 128)
                cells[k, half, :, lanes] = own_ref[k, row]
                cells[k, 1 - half, :, lanes] = other_ref[k, row]
        total[...] = jnp.zeros_like(total)

    products = jnp.dot(
        weight_ref[0], cells[...].reshape(1024, 512), preferred_element_type=F32
    )
    lane = lax.broadcasted_iota(jnp.int32, (64, 128), 1)
    for dy in range(3):
        for z in range(2):
            for y in range(2):
                row = z * 2 + y
                before, centre, after = (
                    products[(dy * 3 + dx) * 64 : (dy * 3 + dx + 1) * 64, row * 128 : (row + 1) * 128]
                    for dx in range(3)
                )
                term = (
                    centre
                    + jnp.where(lane == 0, 0.0, pltpu.roll(before, 1, 1))
                    + jnp.where(lane == 127, 0.0, pltpu.roll(after, 127, 1))
                )
                total[z + 2 - step, y + 2 - dy] += term

    @pl.when(step == 2)
    def _():
        for ref, top, left in ((keep_ref, 0, 0), (y_ref, 0, 2), (z_ref, 2, 0), (corner_ref, 2, 2)):
            for z in range(2):
                for y in range(2):
                    ref[z, y] = total[top + z, left + y]


def convolve(half, own, other, weight):
    whole = lambda shape: pl.BlockSpec(shape, lambda i: (0,) * len(shape))
    return pl.pallas_call(
        conv_kernel,
        grid=(3,),
        in_specs=[SMEM, VMEM, VMEM, pl.BlockSpec((1, 576, 1024), lambda i: (i, 0, 0))],
        out_specs=[whole((2, 2, 64, 128))] * 4,
        out_shape=[jax.ShapeDtypeStruct((2, 2, 64, 128), F32)] * 4,
        scratch_shapes=[pltpu.VMEM((16, 2, 32, 512), BF16), pltpu.VMEM((4, 4, 64, 128), F32)],
        compiler_params=pltpu.CompilerParams(vmem_limit_bytes=16 << 20),
        name="conv",
    )(half, own, other, weight)


def gate_kernel(slot_ref, gz_ref, gy_ref, keep_ref, y_ref, z_ref, corner_ref, out_ref, turned, packed):
    slot = slot_ref[0]
    inside = [jnp.where(ref[0] > 0, 1.0, 0.0) for ref in (gz_ref, gy_ref)]
    group = lax.broadcasted_iota(jnp.int32, (128, 128), 0) // 32
    for z in range(2):
        for y in range(2):
            z_own, z_before = ((inside[0], 1.0), (1.0, inside[0]))[z]
            y_own, y_before = ((inside[1], 1.0), (1.0, inside[1]))[y]
            conv_out = (
                keep_ref[z, y] * (z_own * y_own)
                + y_ref[z, y] * (z_own * y_before)
                + z_ref[z, y] * (z_before * y_own)
                + corner_ref[z, y] * (z_before * y_before)
            )
            gate, value = conv_out[:32], conv_out[32:]
            gated = gate / (1.0 + jnp.exp(-gate)) * value
            spread = jnp.where(group == slot, jnp.concatenate([gated] * 4, axis=0), 0.0)
            turned[...] = spread.T
            for i in range(4):
                packed[pl.ds(i * 4 + z * 2 + y, 32, stride=16), :] = turned[pl.ds(i, 32, stride=4), :]
    out_ref[...] = packed[...].reshape(32, 16, 128).astype(BF16)


def gate(slot, gz, gy, *pieces):
    return pl.pallas_call(
        gate_kernel,
        in_specs=[SMEM] * 3 + [VMEM] * 4,
        out_specs=VMEM,
        out_shape=jax.ShapeDtypeStruct((32, 16, 128), BF16),
        scratch_shapes=[pltpu.VMEM((128, 128), F32), pltpu.VMEM((512, 128), F32)],
        compiler_params=pltpu.CompilerParams(vmem_limit_bytes=4 << 20),
        name="gate",
    )(slot, gz, gy, *pieces)


S, D = (0, 1), (2, 3)


def to_previous(slots):
    even = [slots[4 + S[h]] - 0.25 * (slots[D[h]] + slots[4 + D[h]]) for h in range(2)]
    return slots[:4] + even


def to_next(slots):
    return [slots[4 + D[h]] for h in range(2)]


def project_kernel(gz_ref, gy_ref, parts_ref, proj_ref, own_ref, sent_ref, held, turned):
    chunks = []
    for k in range(8):
        chunk = parts_ref[4 * k].astype(F32)
        for i in range(1, 4):
            chunk = chunk + parts_ref[4 * k + i].astype(F32)
        chunks.append(chunk.astype(BF16))
    held[...] = jnp.dot(
        jnp.concatenate(chunks, axis=1), proj_ref[...], preferred_element_type=F32
    )
    block = lax.broadcasted_iota(jnp.int32, (4, 128), 1) // 32
    for b1 in range(4):
        rows = [held[i * 4 : (i + 1) * 4, b1 * 128 : (b1 + 1) * 128] for i in range(4)]
        hz1, hy1 = b1 // 2, b1 % 2
        for b2 in range(4):
            hz2, hy2 = b2 // 2, b2 % 2
            merged = None
            for i in range(4):
                shift = ((i - b2) % 4) * 32
                moved = rows[i] if shift == 0 else pltpu.roll(rows[i], shift, 1)
                merged = moved if merged is None else jnp.where(block == i, moved, merged)
            for z in range(2):
                for y in range(2):
                    row = merged[z * 2 + y : z * 2 + y + 1, :]
                    z_slot, y_slot = z * 4 + hz1 * 2 + hz2, y * 4 + hy1 * 2 + hy2
                    own_ref[z_slot, y_slot : y_slot + 1, :] = row
                    turned[y_slot, z_slot : z_slot + 1, :] = row

    gz, gy = gz_ref[0], gy_ref[0]
    sent_ref[...] = jnp.zeros_like(sent_ref)

    def send(dz, dy, slots):
        at = ((gz + dz) % 4) * 4 + (gy + dy) % 4
        for k, slot in enumerate(slots):
            sent_ref[at, k] = slot

    by_z = [own_ref[k] for k in range(8)]
    by_y = [turned[k] for k in range(8)]
    for dy in (3, 0, 1):
        send(3, dy, to_previous(by_z))
        send(1, dy, to_next(by_z))
    send(0, 3, to_previous(by_y))
    send(0, 1, to_next(by_y))


def project(gz, gy, parts, proj_weight):
    return pl.pallas_call(
        project_kernel,
        in_specs=[SMEM] * 2 + [VMEM] * 2,
        out_specs=[VMEM] * 2,
        out_shape=[
            jax.ShapeDtypeStruct((8, 8, 128), F32),
            jax.ShapeDtypeStruct((16, 6, 8, 128), F32),
        ],
        scratch_shapes=[pltpu.VMEM((16, 512), F32), pltpu.VMEM((8, 8, 128), F32)],
        compiler_params=pltpu.CompilerParams(vmem_limit_bytes=8 << 20),
        name="project",
    )(gz, gy, parts, proj_weight)


def lift_pair(low, high):
    n = len(low)
    even = [low[i] - 0.25 * (high[i - 1] + high[i]) for i in range(1, n)]
    odd = [high[i] + 0.5 * (even[i - 1] + even[i]) for i in range(1, n - 1)]
    result = []
    for i in range(n - 2):
        result += [even[i], odd[i]]
    return result + [even[n - 2]]


def two_levels(before, own, after):
    middle = []
    for h in range(2):
        low = [own[S[h]], own[4 + S[h]], after[S[h]]]
        high = [before[h], own[D[h]], own[4 + D[h]], after[D[h]]]
        even = [low[i] - 0.25 * (high[i] + high[i + 1]) for i in range(3)] + [after[4 + h]]
        odd = [high[i + 1] + 0.5 * (even[i] + even[i + 1]) for i in range(3)]
        middle.append([odd[0], even[1], odd[1], even[2], odd[2], even[3]])
    return lift_pair(middle[0], middle[1])[:8]


def lift_kernel(gz_ref, gy_ref, own_ref, got_ref, out_ref, across, tall):
    gz, gy = gz_ref[0], gy_ref[0]
    at = lambda dz, dy: ((gz + dz) % 4) * 4 + (gy + dy) % 4
    after, before = at(0, 1), at(0, 3)
    for k in range(6):
        across[1, :, k, :] = got_ref[after, k]
    for k in range(2):
        across[0, :, 6 + k, :] = got_ref[before, k]
    sub = lax.broadcasted_iota(jnp.int32, (8, 128), 0)

    def shortened(cells):
        even = cells - 0.25 * (pltpu.roll(cells, 2, 0) + pltpu.roll(cells, 6, 0))
        return jnp.where(sub < 4, cells, even)

    for side, dy in ((0, 3), (1, 1), (2, 0)):
        change = shortened if side == 1 else lambda cells: cells
        below = [change(got_ref[at(3, dy), k]) for k in range(2)]
        above = [change(got_ref[at(1, dy), k]) for k in range(6)]
        centre = [own_ref[k] if side == 2 else across[side, k] for k in range(8)]
        for i, fine in enumerate(two_levels(below, centre, above)):
            tall[side, :, i, :] = fine
    fine = two_levels(
        [tall[0, 6 + k] for k in range(2)],
        [tall[2, k] for k in range(8)],
        [tall[1, k] for k in range(6)],
    )
    for i in range(8):
        out_ref[:, i, :] = fine[i]


def lift(gz, gy, own, got):
    return pl.pallas_call(
        lift_kernel,
        in_specs=[SMEM] * 2 + [VMEM] * 2,
        out_specs=VMEM,
        out_shape=jax.ShapeDtypeStruct((8, 8, 128), F32),
        scratch_shapes=[pltpu.VMEM((2, 8, 8, 128), F32), pltpu.VMEM((3, 8, 8, 128), F32)],
        compiler_params=pltpu.CompilerParams(vmem_limit_bytes=4 << 20),
        name="lift",
    )(gz, gy, own, got)


def on_device(volume, conv_weight, proj_weight):
    half = lax.axis_index("half")
    slot = ((lax.axis_index("ring") * 2 + half) % 4).reshape(1)
    gz, gy = (lax.axis_index(axis).reshape(1) for axis in ("gz", "gy"))
    own = lax.all_gather(volume.reshape(4, 32, 128), "ring", axis=0, tiled=False)
    other = lax.ppermute(own, "half", [(0, 1), (1, 0)])
    keep, to_y, to_z, to_corner = convolve(
        half.reshape(1), own, other, conv_weight.reshape(3, 576, 1024)
    )
    step = [(i, (i + 1) % 4) for i in range(4)]
    both = [(a * 4 + b, c * 4 + d) for a, c in step for b, d in step]
    sent = gate(
        slot,
        gz,
        gy,
        keep,
        lax.ppermute(to_y, "gy", step),
        lax.ppermute(to_z, "gz", step),
        lax.ppermute(to_corner, ("gz", "gy"), both),
    )
    parts = lax.all_to_all(sent, ("ring", "half"), split_axis=0, concat_axis=0, tiled=True)
    coefficients, messages = project(gz, gy, parts, proj_weight)
    got = lax.all_to_all(messages, ("gz", "gy"), split_axis=0, concat_axis=0, tiled=True)
    return lift(gz, gy, coefficients, got)


def solution(mesh):
    split = Mesh(mesh.devices.reshape(4, 4, 16, 2), ("gz", "gy", "ring", "half"))
    col = ("ring", "half")
    return jax.shard_map(
        on_device,
        mesh=split,
        in_specs=(P("gz", "gy", col, None), P(None, None, col, None), P()),
        out_specs=P("gz", "gy", col),
        check_vma=False,
    )
```

```python
import jax
import jax.numpy as jnp
from jax import lax
from jax.experimental import pallas as pl
from jax.experimental.pallas import tpu as pltpu
from jax.sharding import Mesh, PartitionSpec as P

F32 = jnp.float32
BF16 = jnp.bfloat16
VMEM = pl.BlockSpec(memory_space=pltpu.VMEM)
SMEM = pl.BlockSpec(memory_space=pltpu.SMEM)


def split_kernel(own_ref, first_ref, second_ref):
    first_ref[...] = own_ref[:8]
    second_ref[...] = own_ref[8:]


def split(own):
    piece = jax.ShapeDtypeStruct((8, 4, 32, 128), BF16)
    return pl.pallas_call(
        split_kernel,
        in_specs=[VMEM],
        out_specs=[VMEM] * 2,
        out_shape=[piece] * 2,
        compiler_params=pltpu.CompilerParams(vmem_limit_bytes=4 << 20),
        cost_estimate=pl.CostEstimate(flops=0, bytes_accessed=1 << 20, transcendentals=0),
        name="split",
    )(own)


ORDER = (0, 2, 1, 3)


def place_of(k):
    return 4 * (k // 4) + ORDER.index(k % 4)


def spread_terms(products, lane):
    for dy in range(3):
        for z in range(2):
            for y in range(2):
                row = z * 2 + y
                before, centre, after = (
                    products[(dy * 3 + dx) * 64 : (dy * 3 + dx + 1) * 64, row * 128 : (row + 1) * 128]
                    for dx in range(3)
                )
                yield z + 2, y + 2 - dy, (
                    centre
                    + jnp.where(lane == 0, 0.0, pltpu.roll(before, 1, 1))
                    + jnp.where(lane == 127, 0.0, pltpu.roll(after, 127, 1))
                )


def own_half_kernel(half_ref, own_ref, weight_ref, total_ref, rest_ref, cells, mine):
    step = pl.program_id(0)

    @pl.when(step == 0)
    def _():
        for k in range(16):
            for row in range(4):
                cells[place_of(k), :, row * 128 : (row + 1) * 128] = own_ref[k, row]
        total_ref[...] = jnp.zeros_like(total_ref)

    lane = lax.broadcasted_iota(jnp.int32, (64, 128), 1)
    first = half_ref[0] == 0
    for r in range(9):
        rows = slice(r * 64, (r + 1) * 64)
        for u in range(4):
            left = weight_ref[0, rows, u * 256 : u * 256 + 128].astype(F32)
            right = weight_ref[0, rows, u * 256 + 128 : (u + 1) * 256].astype(F32)
            keep = lane // 32 % 2 == 0
            even = jnp.where(keep, left, pltpu.roll(right, 32, 1)).astype(BF16)
            odd = jnp.where(keep, pltpu.roll(left, 96, 1), right).astype(BF16)
            mine[rows, u * 128 : (u + 1) * 128] = jnp.where(first, even, odd)
            rest_ref[0, rows, u * 128 : (u + 1) * 128] = jnp.where(first, odd, even)

    products = jnp.dot(mine[...], cells[...].reshape(512, 512), preferred_element_type=F32)
    for z, y, term in spread_terms(products, lane):
        total_ref[z - step, y] += term


def own_half(half, own, weight):
    return pl.pallas_call(
        own_half_kernel,
        grid=(3,),
        in_specs=[SMEM, VMEM, pl.BlockSpec((1, 576, 1024), lambda i: (i, 0, 0))],
        out_specs=[
            pl.BlockSpec((4, 4, 64, 128), lambda i: (0, 0, 0, 0)),
            pl.BlockSpec((1, 576, 512), lambda i: (i, 0, 0)),
        ],
        out_shape=[
            jax.ShapeDtypeStruct((4, 4, 64, 128), F32),
            jax.ShapeDtypeStruct((3, 576, 512), BF16),
        ],
        scratch_shapes=[pltpu.VMEM((16, 32, 512), BF16), pltpu.VMEM((576, 512), BF16)],
        compiler_params=pltpu.CompilerParams(vmem_limit_bytes=16 << 20),
        cost_estimate=pl.CostEstimate(flops=1 << 30, bytes_accessed=6 << 20, transcendentals=0),
        name="own_half",
    )(half, own, weight)


def other_half_kernel(first_ref, second_ref, rest_ref, total_ref, keep_ref, y_ref, z_ref, corner_ref, cells):
    for k in range(16):
        for row in range(4):
            cells[place_of(k), :, row * 128 : (row + 1) * 128] = (first_ref, second_ref)[k // 8][k % 8, row]
    sums = ((keep_ref, y_ref), (z_ref, corner_ref))
    for z in range(4):
        for y in range(4):
            sums[z // 2][y // 2][z % 2, y % 2] = total_ref[z, y]
    lane = lax.broadcasted_iota(jnp.int32, (64, 128), 1)
    for step in range(3):
        products = jnp.dot(rest_ref[step], cells[...].reshape(512, 512), preferred_element_type=F32)
        for z, y, term in spread_terms(products, lane):
            z = z - step
            sums[z // 2][y // 2][z % 2, y % 2] += term


def other_half(first, second, rest, total):
    return pl.pallas_call(
        other_half_kernel,
        in_specs=[VMEM] * 4,
        out_specs=[VMEM] * 4,
        out_shape=[jax.ShapeDtypeStruct((2, 2, 64, 128), F32)] * 4,
        scratch_shapes=[pltpu.VMEM((16, 32, 512), BF16)],
        compiler_params=pltpu.CompilerParams(vmem_limit_bytes=16 << 20),
        cost_estimate=pl.CostEstimate(flops=1 << 30, bytes_accessed=3 << 20, transcendentals=0),
        name="other_half",
    )(first, second, rest, total)


def gate_kernel(slot_ref, gz_ref, gy_ref, keep_ref, y_ref, z_ref, corner_ref, out_ref, turned, packed):
    slot = slot_ref[0]
    inside = [jnp.where(ref[0] > 0, 1.0, 0.0) for ref in (gz_ref, gy_ref)]
    group = lax.broadcasted_iota(jnp.int32, (128, 128), 0) // 32
    for z in range(2):
        for y in range(2):
            z_own, z_before = ((inside[0], 1.0), (1.0, inside[0]))[z]
            y_own, y_before = ((inside[1], 1.0), (1.0, inside[1]))[y]
            conv_out = (
                keep_ref[z, y] * (z_own * y_own)
                + y_ref[z, y] * (z_own * y_before)
                + z_ref[z, y] * (z_before * y_own)
                + corner_ref[z, y] * (z_before * y_before)
            )
            gate, value = conv_out[:32], conv_out[32:]
            gated = gate / (1.0 + jnp.exp(-gate)) * value
            spread = jnp.where(group == slot, jnp.concatenate([gated] * 4, axis=0), 0.0)
            turned[...] = spread.T
            for i in range(4):
                packed[pl.ds(i * 4 + z * 2 + y, 32, stride=16), :] = turned[pl.ds(i, 32, stride=4), :]
    out_ref[...] = packed[...].reshape(32, 16, 128).astype(BF16)


def gate(slot, gz, gy, *pieces):
    return pl.pallas_call(
        gate_kernel,
        in_specs=[SMEM] * 3 + [VMEM] * 4,
        out_specs=VMEM,
        out_shape=jax.ShapeDtypeStruct((32, 16, 128), BF16),
        scratch_shapes=[pltpu.VMEM((128, 128), F32), pltpu.VMEM((512, 128), F32)],
        compiler_params=pltpu.CompilerParams(vmem_limit_bytes=4 << 20),
        name="gate",
    )(slot, gz, gy, *pieces)


S, D = (0, 1), (2, 3)


def to_previous(slots):
    even = [slots[4 + S[h]] - 0.25 * (slots[D[h]] + slots[4 + D[h]]) for h in range(2)]
    return slots[:4] + even


def to_next(slots):
    return [slots[4 + D[h]] for h in range(2)]


def project_kernel(gz_ref, gy_ref, parts_ref, proj_ref, own_ref, sent_ref, held, turned):
    chunks = []
    for k in range(8):
        chunk = parts_ref[4 * k].astype(F32)
        for i in range(1, 4):
            chunk = chunk + parts_ref[4 * k + i].astype(F32)
        chunks.append(chunk.astype(BF16))
    held[...] = jnp.dot(
        jnp.concatenate(chunks, axis=1), proj_ref[...], preferred_element_type=F32
    )
    block = lax.broadcasted_iota(jnp.int32, (4, 128), 1) // 32
    for b1 in range(4):
        rows = [held[i * 4 : (i + 1) * 4, b1 * 128 : (b1 + 1) * 128] for i in range(4)]
        hz1, hy1 = b1 // 2, b1 % 2
        for b2 in range(4):
            hz2, hy2 = b2 // 2, b2 % 2
            merged = None
            for i in range(4):
                shift = ((i - b2) % 4) * 32
                moved = rows[i] if shift == 0 else pltpu.roll(rows[i], shift, 1)
                merged = moved if merged is None else jnp.where(block == i, moved, merged)
            for z in range(2):
                for y in range(2):
                    row = merged[z * 2 + y : z * 2 + y + 1, :]
                    z_slot, y_slot = z * 4 + hz1 * 2 + hz2, y * 4 + hy1 * 2 + hy2
                    own_ref[z_slot, y_slot : y_slot + 1, :] = row
                    turned[y_slot, z_slot : z_slot + 1, :] = row

    gz, gy = gz_ref[0], gy_ref[0]
    sent_ref[...] = jnp.zeros_like(sent_ref)

    def send(dz, dy, slots):
        at = ((gz + dz) % 4) * 4 + (gy + dy) % 4
        for k in range(len(slots) // 2):
            sent_ref[at, k] = jnp.concatenate(slots[2 * k : 2 * k + 2], axis=0).astype(BF16)

    by_z = [own_ref[k] for k in range(8)]
    by_y = [turned[k] for k in range(8)]
    for dy in (3, 0, 1):
        send(3, dy, to_previous(by_z))
        send(1, dy, to_next(by_z))
    send(0, 3, to_previous(by_y))
    send(0, 1, to_next(by_y))


def project(gz, gy, parts, proj_weight):
    return pl.pallas_call(
        project_kernel,
        in_specs=[SMEM] * 2 + [VMEM] * 2,
        out_specs=[VMEM] * 2,
        out_shape=[
            jax.ShapeDtypeStruct((8, 8, 128), F32),
            jax.ShapeDtypeStruct((16, 3, 16, 128), BF16),
        ],
        scratch_shapes=[pltpu.VMEM((16, 512), F32), pltpu.VMEM((8, 8, 128), F32)],
        compiler_params=pltpu.CompilerParams(vmem_limit_bytes=8 << 20),
        name="project",
    )(gz, gy, parts, proj_weight)


def lift_pair(low, high):
    n = len(low)
    even = [low[i] - 0.25 * (high[i - 1] + high[i]) for i in range(1, n)]
    odd = [high[i] + 0.5 * (even[i - 1] + even[i]) for i in range(1, n - 1)]
    result = []
    for i in range(n - 2):
        result += [even[i], odd[i]]
    return result + [even[n - 2]]


def two_levels(before, own, after):
    middle = []
    for h in range(2):
        low = [own[S[h]], own[4 + S[h]], after[S[h]]]
        high = [before[h], own[D[h]], own[4 + D[h]], after[D[h]]]
        even = [low[i] - 0.25 * (high[i] + high[i + 1]) for i in range(3)] + [after[4 + h]]
        odd = [high[i + 1] + 0.5 * (even[i] + even[i + 1]) for i in range(3)]
        middle.append([odd[0], even[1], odd[1], even[2], odd[2], even[3]])
    return lift_pair(middle[0], middle[1])[:8]


def lift_kernel(gz_ref, gy_ref, own_ref, got_ref, out_ref, across, tall):
    gz, gy = gz_ref[0], gy_ref[0]
    at = lambda dz, dy: ((gz + dz) % 4) * 4 + (gy + dy) % 4
    after, before = at(0, 1), at(0, 3)

    def slots_from(source, count):
        for k in range(count // 2):
            pair = got_ref[source, k].astype(F32)
            yield pair[:8]
            yield pair[8:]

    for k, cells in enumerate(slots_from(after, 6)):
        across[1, :, k, :] = cells
    for k, cells in enumerate(slots_from(before, 2)):
        across[0, :, 6 + k, :] = cells
    sub = lax.broadcasted_iota(jnp.int32, (8, 128), 0)

    def shortened(cells):
        even = cells - 0.25 * (pltpu.roll(cells, 2, 0) + pltpu.roll(cells, 6, 0))
        return jnp.where(sub < 4, cells, even)

    for side, dy in ((0, 3), (1, 1), (2, 0)):
        change = shortened if side == 1 else lambda cells: cells
        below = [change(cells) for cells in slots_from(at(3, dy), 2)]
        above = [change(cells) for cells in slots_from(at(1, dy), 6)]
        centre = [own_ref[k] if side == 2 else across[side, k] for k in range(8)]
        for i, fine in enumerate(two_levels(below, centre, above)):
            tall[side, :, i, :] = fine
    fine = two_levels(
        [tall[0, 6 + k] for k in range(2)],
        [tall[2, k] for k in range(8)],
        [tall[1, k] for k in range(6)],
    )
    for i in range(8):
        out_ref[:, i, :] = fine[i]


def lift(gz, gy, own, got):
    return pl.pallas_call(
        lift_kernel,
        in_specs=[SMEM] * 2 + [VMEM] * 2,
        out_specs=VMEM,
        out_shape=jax.ShapeDtypeStruct((8, 8, 128), F32),
        scratch_shapes=[pltpu.VMEM((2, 8, 8, 128), F32), pltpu.VMEM((3, 8, 8, 128), F32)],
        compiler_params=pltpu.CompilerParams(vmem_limit_bytes=4 << 20),
        name="lift",
    )(gz, gy, own, got)


def on_device(volume, conv_weight, proj_weight):
    half = lax.axis_index("half")
    slot = ((lax.axis_index("ring") * 2 + half) % 4).reshape(1)
    gz, gy = (lax.axis_index(axis).reshape(1) for axis in ("gz", "gy"))
    own = lax.all_gather(volume.reshape(4, 32, 128), "ring", axis=0, tiled=False)
    swapped = [lax.ppermute(piece, "half", [(0, 1), (1, 0)]) for piece in split(own)]
    total, rest = own_half(half.reshape(1), own, conv_weight.reshape(3, 576, 1024))
    keep, to_y, to_z, to_corner = other_half(*swapped, rest, total)
    step = [(i, (i + 1) % 4) for i in range(4)]
    both = [(a * 4 + b, c * 4 + d) for a, c in step for b, d in step]
    sent = gate(
        slot,
        gz,
        gy,
        keep,
        lax.ppermute(to_y, "gy", step),
        lax.ppermute(to_z, "gz", step),
        lax.ppermute(to_corner, ("gz", "gy"), both),
    )
    parts = lax.all_to_all(sent, ("ring", "half"), split_axis=0, concat_axis=0, tiled=True)
    coefficients, messages = project(gz, gy, parts, proj_weight)
    got = lax.all_to_all(messages, ("gz", "gy"), split_axis=0, concat_axis=0, tiled=True)
    return lift(gz, gy, coefficients, got)


def solution(mesh):
    split = Mesh(mesh.devices.reshape(4, 4, 16, 2), ("gz", "gy", "ring", "half"))
    col = ("ring", "half")
    return jax.shard_map(
        on_device,
        mesh=split,
        in_specs=(P("gz", "gy", col, None), P(None, None, col, None), P()),
        out_specs=P("gz", "gy", col),
        check_vma=False,
    )
```

```python
import jax
import jax.numpy as jnp
from jax import lax
from jax.experimental import pallas as pl
from jax.experimental.pallas import tpu as pltpu
from jax.sharding import Mesh, PartitionSpec as P

F32 = jnp.float32
BF16 = jnp.bfloat16
VMEM = pl.BlockSpec(memory_space=pltpu.VMEM)
SMEM = pl.BlockSpec(memory_space=pltpu.SMEM)


ORDER = (0, 2, 1, 3)


def place_of(k):
    return 4 * (k // 4) + ORDER.index(k % 4)


def spread_terms(products, lane):
    for dy in range(3):
        for z in range(2):
            for y in range(2):
                row = z * 2 + y
                before, centre, after = (
                    products[(dy * 3 + dx) * 64 : (dy * 3 + dx + 1) * 64, row * 128 : (row + 1) * 128]
                    for dx in range(3)
                )
                yield z + 2, y + 2 - dy, (
                    centre
                    + jnp.where(lane == 0, 0.0, pltpu.roll(before, 1, 1))
                    + jnp.where(lane == 127, 0.0, pltpu.roll(after, 127, 1))
                )


def own_half_kernel(half_ref, own_ref, weight_ref, total_ref, rest_ref, cells, mine):
    step = pl.program_id(0)

    @pl.when(step == 0)
    def _():
        for k in range(16):
            for row in range(4):
                cells[place_of(k), :, row * 128 : (row + 1) * 128] = own_ref[k, row]
        total_ref[...] = jnp.zeros_like(total_ref)

    lane = lax.broadcasted_iota(jnp.int32, (64, 128), 1)
    first = half_ref[0] == 0
    for r in range(9):
        rows = slice(r * 64, (r + 1) * 64)
        for u in range(4):
            left = weight_ref[0, rows, u * 256 : u * 256 + 128].astype(F32)
            right = weight_ref[0, rows, u * 256 + 128 : (u + 1) * 256].astype(F32)
            keep = lane // 32 % 2 == 0
            even = jnp.where(keep, left, pltpu.roll(right, 32, 1)).astype(BF16)
            odd = jnp.where(keep, pltpu.roll(left, 96, 1), right).astype(BF16)
            mine[rows, u * 128 : (u + 1) * 128] = jnp.where(first, even, odd)
            rest_ref[0, rows, u * 128 : (u + 1) * 128] = jnp.where(first, odd, even)

    products = jnp.dot(mine[...], cells[...].reshape(512, 512), preferred_element_type=F32)
    for z, y, term in spread_terms(products, lane):
        total_ref[z - step, y] += term


def own_half(half, own, weight):
    return pl.pallas_call(
        own_half_kernel,
        grid=(3,),
        in_specs=[SMEM, VMEM, pl.BlockSpec((1, 576, 1024), lambda i: (i, 0, 0))],
        out_specs=[
            pl.BlockSpec((4, 4, 64, 128), lambda i: (0, 0, 0, 0)),
            pl.BlockSpec((1, 576, 512), lambda i: (i, 0, 0)),
        ],
        out_shape=[
            jax.ShapeDtypeStruct((4, 4, 64, 128), F32),
            jax.ShapeDtypeStruct((3, 576, 512), BF16),
        ],
        scratch_shapes=[pltpu.VMEM((16, 32, 512), BF16), pltpu.VMEM((576, 512), BF16)],
        compiler_params=pltpu.CompilerParams(vmem_limit_bytes=16 << 20),
        cost_estimate=pl.CostEstimate(flops=1 << 30, bytes_accessed=6 << 20, transcendentals=0),
        name="own_half",
    )(half, own, weight)


def other_half_kernel(other_ref, rest_ref, total_ref, keep_ref, y_ref, z_ref, corner_ref, cells):
    for k in range(16):
        for row in range(4):
            cells[place_of(k), :, row * 128 : (row + 1) * 128] = other_ref[k, row]
    sums = ((keep_ref, y_ref), (z_ref, corner_ref))
    for z in range(4):
        for y in range(4):
            sums[z // 2][y // 2][z % 2, y % 2] = total_ref[z, y]
    lane = lax.broadcasted_iota(jnp.int32, (64, 128), 1)
    for step in range(3):
        products = jnp.dot(rest_ref[step], cells[...].reshape(512, 512), preferred_element_type=F32)
        for z, y, term in spread_terms(products, lane):
            z = z - step
            sums[z // 2][y // 2][z % 2, y % 2] += term


def other_half(other, rest, total):
    return pl.pallas_call(
        other_half_kernel,
        in_specs=[VMEM] * 3,
        out_specs=[VMEM] * 4,
        out_shape=[jax.ShapeDtypeStruct((2, 2, 64, 128), F32)] * 4,
        scratch_shapes=[pltpu.VMEM((16, 32, 512), BF16)],
        compiler_params=pltpu.CompilerParams(vmem_limit_bytes=16 << 20),
        cost_estimate=pl.CostEstimate(flops=1 << 30, bytes_accessed=3 << 20, transcendentals=0),
        name="other_half",
    )(other, rest, total)


def gate_kernel(slot_ref, gz_ref, gy_ref, keep_ref, y_ref, z_ref, corner_ref, out_ref, turned, packed):
    slot = slot_ref[0]
    inside = [jnp.where(ref[0] > 0, 1.0, 0.0) for ref in (gz_ref, gy_ref)]
    group = lax.broadcasted_iota(jnp.int32, (128, 128), 0) // 32
    for z in range(2):
        for y in range(2):
            z_own, z_before = ((inside[0], 1.0), (1.0, inside[0]))[z]
            y_own, y_before = ((inside[1], 1.0), (1.0, inside[1]))[y]
            conv_out = (
                keep_ref[z, y] * (z_own * y_own)
                + y_ref[z, y] * (z_own * y_before)
                + z_ref[z, y] * (z_before * y_own)
                + corner_ref[z, y] * (z_before * y_before)
            )
            gate, value = conv_out[:32], conv_out[32:]
            gated = gate / (1.0 + jnp.exp(-gate)) * value
            spread = jnp.where(group == slot, jnp.concatenate([gated] * 4, axis=0), 0.0)
            turned[...] = spread.T
            for i in range(4):
                packed[pl.ds(i * 4 + z * 2 + y, 32, stride=16), :] = turned[pl.ds(i, 32, stride=4), :]
    out_ref[...] = packed[...].reshape(32, 16, 128).astype(BF16)


def gate(slot, gz, gy, *pieces):
    return pl.pallas_call(
        gate_kernel,
        in_specs=[SMEM] * 3 + [VMEM] * 4,
        out_specs=VMEM,
        out_shape=jax.ShapeDtypeStruct((32, 16, 128), BF16),
        scratch_shapes=[pltpu.VMEM((128, 128), F32), pltpu.VMEM((512, 128), F32)],
        compiler_params=pltpu.CompilerParams(vmem_limit_bytes=4 << 20),
        name="gate",
    )(slot, gz, gy, *pieces)


S, D = (0, 1), (2, 3)


def to_previous(slots):
    even = [slots[4 + S[h]] - 0.25 * (slots[D[h]] + slots[4 + D[h]]) for h in range(2)]
    return slots[:4] + even


def to_next(slots):
    return [slots[4 + D[h]] for h in range(2)]


def project_kernel(gz_ref, gy_ref, parts_ref, proj_ref, own_ref, sent_ref, held, turned):
    chunks = []
    for k in range(8):
        chunk = parts_ref[4 * k].astype(F32)
        for i in range(1, 4):
            chunk = chunk + parts_ref[4 * k + i].astype(F32)
        chunks.append(chunk.astype(BF16))
    held[...] = jnp.dot(
        jnp.concatenate(chunks, axis=1), proj_ref[...], preferred_element_type=F32
    )
    block = lax.broadcasted_iota(jnp.int32, (4, 128), 1) // 32
    for b1 in range(4):
        rows = [held[i * 4 : (i + 1) * 4, b1 * 128 : (b1 + 1) * 128] for i in range(4)]
        hz1, hy1 = b1 // 2, b1 % 2
        for b2 in range(4):
            hz2, hy2 = b2 // 2, b2 % 2
            merged = None
            for i in range(4):
                shift = ((i - b2) % 4) * 32
                moved = rows[i] if shift == 0 else pltpu.roll(rows[i], shift, 1)
                merged = moved if merged is None else jnp.where(block == i, moved, merged)
            for z in range(2):
                for y in range(2):
                    row = merged[z * 2 + y : z * 2 + y + 1, :]
                    z_slot, y_slot = z * 4 + hz1 * 2 + hz2, y * 4 + hy1 * 2 + hy2
                    own_ref[z_slot, y_slot : y_slot + 1, :] = row
                    turned[y_slot, z_slot : z_slot + 1, :] = row

    gz, gy = gz_ref[0], gy_ref[0]
    sent_ref[...] = jnp.zeros_like(sent_ref)

    def send(dz, dy, slots):
        at = ((gz + dz) % 4) * 4 + (gy + dy) % 4
        for k in range(len(slots) // 2):
            sent_ref[at, k] = jnp.concatenate(slots[2 * k : 2 * k + 2], axis=0).astype(BF16)

    by_z = [own_ref[k] for k in range(8)]
    by_y = [turned[k] for k in range(8)]
    for dy in (3, 0, 1):
        send(3, dy, to_previous(by_z))
        send(1, dy, to_next(by_z))
    send(0, 3, to_previous(by_y))
    send(0, 1, to_next(by_y))


def project(gz, gy, parts, proj_weight):
    return pl.pallas_call(
        project_kernel,
        in_specs=[SMEM] * 2 + [VMEM] * 2,
        out_specs=[VMEM] * 2,
        out_shape=[
            jax.ShapeDtypeStruct((8, 8, 128), F32),
            jax.ShapeDtypeStruct((16, 3, 16, 128), BF16),
        ],
        scratch_shapes=[pltpu.VMEM((16, 512), F32), pltpu.VMEM((8, 8, 128), F32)],
        compiler_params=pltpu.CompilerParams(vmem_limit_bytes=8 << 20),
        name="project",
    )(gz, gy, parts, proj_weight)


def lift_pair(low, high):
    n = len(low)
    even = [low[i] - 0.25 * (high[i - 1] + high[i]) for i in range(1, n)]
    odd = [high[i] + 0.5 * (even[i - 1] + even[i]) for i in range(1, n - 1)]
    result = []
    for i in range(n - 2):
        result += [even[i], odd[i]]
    return result + [even[n - 2]]


def two_levels(before, own, after):
    middle = []
    for h in range(2):
        low = [own[S[h]], own[4 + S[h]], after[S[h]]]
        high = [before[h], own[D[h]], own[4 + D[h]], after[D[h]]]
        even = [low[i] - 0.25 * (high[i] + high[i + 1]) for i in range(3)] + [after[4 + h]]
        odd = [high[i + 1] + 0.5 * (even[i] + even[i + 1]) for i in range(3)]
        middle.append([odd[0], even[1], odd[1], even[2], odd[2], even[3]])
    return lift_pair(middle[0], middle[1])[:8]


def lift_kernel(gz_ref, gy_ref, own_ref, got_ref, out_ref, across, tall):
    gz, gy = gz_ref[0], gy_ref[0]
    at = lambda dz, dy: ((gz + dz) % 4) * 4 + (gy + dy) % 4
    after, before = at(0, 1), at(0, 3)

    def slots_from(source, count):
        for k in range(count // 2):
            pair = got_ref[source, k].astype(F32)
            yield pair[:8]
            yield pair[8:]

    for k, cells in enumerate(slots_from(after, 6)):
        across[1, :, k, :] = cells
    for k, cells in enumerate(slots_from(before, 2)):
        across[0, :, 6 + k, :] = cells
    sub = lax.broadcasted_iota(jnp.int32, (8, 128), 0)

    def shortened(cells):
        even = cells - 0.25 * (pltpu.roll(cells, 2, 0) + pltpu.roll(cells, 6, 0))
        return jnp.where(sub < 4, cells, even)

    for side, dy in ((0, 3), (1, 1), (2, 0)):
        change = shortened if side == 1 else lambda cells: cells
        below = [change(cells) for cells in slots_from(at(3, dy), 2)]
        above = [change(cells) for cells in slots_from(at(1, dy), 6)]
        centre = [own_ref[k] if side == 2 else across[side, k] for k in range(8)]
        for i, fine in enumerate(two_levels(below, centre, above)):
            tall[side, :, i, :] = fine
    fine = two_levels(
        [tall[0, 6 + k] for k in range(2)],
        [tall[2, k] for k in range(8)],
        [tall[1, k] for k in range(6)],
    )
    for i in range(8):
        out_ref[:, i, :] = fine[i]


def lift(gz, gy, own, got):
    return pl.pallas_call(
        lift_kernel,
        in_specs=[SMEM] * 2 + [VMEM] * 2,
        out_specs=VMEM,
        out_shape=jax.ShapeDtypeStruct((8, 8, 128), F32),
        scratch_shapes=[pltpu.VMEM((2, 8, 8, 128), F32), pltpu.VMEM((3, 8, 8, 128), F32)],
        compiler_params=pltpu.CompilerParams(vmem_limit_bytes=4 << 20),
        name="lift",
    )(gz, gy, own, got)


def on_device(volume, conv_weight, proj_weight):
    half = lax.axis_index("half")
    slot = ((lax.axis_index("ring") * 2 + half) % 4).reshape(1)
    gz, gy = (lax.axis_index(axis).reshape(1) for axis in ("gz", "gy"))
    copies = jnp.broadcast_to(volume.reshape(1, 4, 32, 128), (16, 4, 32, 128))
    own = lax.all_to_all(copies, "ring", split_axis=0, concat_axis=0, tiled=True)
    other = lax.ppermute(own, "half", [(0, 1), (1, 0)])
    total, rest = own_half(half.reshape(1), own, conv_weight.reshape(3, 576, 1024))
    keep, to_y, to_z, to_corner = other_half(other, rest, total)
    step = [(i, (i + 1) % 4) for i in range(4)]
    both = [(a * 4 + b, c * 4 + d) for a, c in step for b, d in step]
    sent = gate(
        slot,
        gz,
        gy,
        keep,
        lax.ppermute(to_y, "gy", step),
        lax.ppermute(to_z, "gz", step),
        lax.ppermute(to_corner, ("gz", "gy"), both),
    )
    parts = lax.all_to_all(sent, ("ring", "half"), split_axis=0, concat_axis=0, tiled=True)
    coefficients, messages = project(gz, gy, parts, proj_weight)
    got = lax.all_to_all(messages, ("gz", "gy"), split_axis=0, concat_axis=0, tiled=True)
    return lift(gz, gy, coefficients, got)


def solution(mesh):
    split = Mesh(mesh.devices.reshape(4, 4, 16, 2), ("gz", "gy", "ring", "half"))
    col = ("ring", "half")
    return jax.shard_map(
        on_device,
        mesh=split,
        in_specs=(P("gz", "gy", col, None), P(None, None, col, None), P()),
        out_specs=P("gz", "gy", col),
        check_vma=False,
    )
```

```python
import jax
import jax.numpy as jnp
from jax import lax
from jax.experimental import pallas as pl
from jax.experimental.pallas import tpu as pltpu
from jax.sharding import Mesh, PartitionSpec as P


F32 = jnp.float32
BF16 = jnp.bfloat16
VMEM = pl.BlockSpec(memory_space=pltpu.VMEM)
SMEM = pl.BlockSpec(memory_space=pltpu.SMEM)


ORDER = (0, 2, 1, 3)


def place_of(k):
    return 4 * (k // 4) + ORDER.index(k % 4)


def spread_terms(products, lane):
    for dy in range(3):
        for z in range(2):
            for y in range(2):
                row = z * 2 + y
                before, centre, after = (
                    products[(dy * 3 + dx) * 64 : (dy * 3 + dx + 1) * 64, row * 128 : (row + 1) * 128]
                    for dx in range(3)
                )
                yield z + 2, y + 2 - dy, (
                    centre
                    + jnp.where(lane == 0, 0.0, pltpu.roll(before, 1, 1))
                    + jnp.where(lane == 127, 0.0, pltpu.roll(after, 127, 1))
                )


def own_half_kernel(half_ref, own_ref, weight_ref, total_ref, rest_ref, cells, mine):
    step = pl.program_id(0)

    @pl.when(step == 0)
    def _():
        for k in range(16):
            for row in range(4):
                cells[place_of(k), :, row * 128 : (row + 1) * 128] = own_ref[k, row]
        total_ref[...] = jnp.zeros_like(total_ref)

    lane = lax.broadcasted_iota(jnp.int32, (64, 128), 1)
    first = half_ref[0] == 0
    for r in range(9):
        rows = slice(r * 64, (r + 1) * 64)
        for u in range(4):
            left = weight_ref[0, rows, u * 256 : u * 256 + 128].astype(F32)
            right = weight_ref[0, rows, u * 256 + 128 : (u + 1) * 256].astype(F32)
            keep = lane // 32 % 2 == 0
            even = jnp.where(keep, left, pltpu.roll(right, 32, 1)).astype(BF16)
            odd = jnp.where(keep, pltpu.roll(left, 96, 1), right).astype(BF16)
            mine[rows, u * 128 : (u + 1) * 128] = jnp.where(first, even, odd)
            rest_ref[0, rows, u * 128 : (u + 1) * 128] = jnp.where(first, odd, even)

    products = jnp.dot(mine[...], cells[...].reshape(512, 512), preferred_element_type=F32)
    for z, y, term in spread_terms(products, lane):
        total_ref[z - step, y] += term


def own_half(half, own, weight):
    return pl.pallas_call(
        own_half_kernel,
        grid=(3,),
        in_specs=[SMEM, VMEM, pl.BlockSpec((1, 576, 1024), lambda i: (i, 0, 0))],
        out_specs=[
            pl.BlockSpec((4, 4, 64, 128), lambda i: (0, 0, 0, 0)),
            pl.BlockSpec((1, 576, 512), lambda i: (i, 0, 0)),
        ],
        out_shape=[
            jax.ShapeDtypeStruct((4, 4, 64, 128), F32),
            jax.ShapeDtypeStruct((3, 576, 512), BF16),
        ],
        scratch_shapes=[pltpu.VMEM((16, 32, 512), BF16), pltpu.VMEM((576, 512), BF16)],
        compiler_params=pltpu.CompilerParams(vmem_limit_bytes=16 << 20),
        cost_estimate=pl.CostEstimate(flops=1 << 30, bytes_accessed=6 << 20, transcendentals=0),
        name="own_half",
    )(half, own, weight)


def other_half_kernel(other_ref, rest_ref, total_ref, keep_ref, y_ref, z_ref, corner_ref, cells):
    for k in range(16):
        for row in range(4):
            cells[place_of(k), :, row * 128 : (row + 1) * 128] = other_ref[k, row]
    sums = ((keep_ref, y_ref), (z_ref, corner_ref))
    for z in range(4):
        for y in range(4):
            sums[z // 2][y // 2][z % 2, y % 2] = total_ref[z, y]
    lane = lax.broadcasted_iota(jnp.int32, (64, 128), 1)
    for step in range(3):
        products = jnp.dot(rest_ref[step], cells[...].reshape(512, 512), preferred_element_type=F32)
        for z, y, term in spread_terms(products, lane):
            z = z - step
            sums[z // 2][y // 2][z % 2, y % 2] += term


def other_half(other, rest, total):
    return pl.pallas_call(
        other_half_kernel,
        in_specs=[VMEM] * 3,
        out_specs=[VMEM] * 4,
        out_shape=[jax.ShapeDtypeStruct((2, 2, 64, 128), F32)] * 4,
        scratch_shapes=[pltpu.VMEM((16, 32, 512), BF16)],
        compiler_params=pltpu.CompilerParams(vmem_limit_bytes=16 << 20),
        cost_estimate=pl.CostEstimate(flops=1 << 30, bytes_accessed=3 << 20, transcendentals=0),
        name="other_half",
    )(other, rest, total)


def gate_kernel(slot_ref, gz_ref, gy_ref, keep_ref, y_ref, z_ref, corner_ref, out_ref, turned, packed):
    slot = slot_ref[0]
    inside = [jnp.where(ref[0] > 0, 1.0, 0.0) for ref in (gz_ref, gy_ref)]
    group = lax.broadcasted_iota(jnp.int32, (128, 128), 0) // 32
    for z in range(2):
        for y in range(2):
            z_own, z_before = ((inside[0], 1.0), (1.0, inside[0]))[z]
            y_own, y_before = ((inside[1], 1.0), (1.0, inside[1]))[y]
            conv_out = (
                keep_ref[z, y] * (z_own * y_own)
                + y_ref[z, y] * (z_own * y_before)
                + z_ref[z, y] * (z_before * y_own)
                + corner_ref[z, y] * (z_before * y_before)
            )
            gate, value = conv_out[:32], conv_out[32:]
            gated = gate / (1.0 + jnp.exp(-gate)) * value
            spread = jnp.where(group == slot, jnp.concatenate([gated] * 4, axis=0), 0.0)
            turned[...] = spread.T
            for i in range(4):
                packed[pl.ds(i * 4 + z * 2 + y, 32, stride=16), :] = turned[pl.ds(i, 32, stride=4), :]
    out_ref[...] = packed[...].reshape(32, 16, 128).astype(BF16)


def gate(slot, gz, gy, *pieces):
    return pl.pallas_call(
        gate_kernel,
        in_specs=[SMEM] * 3 + [VMEM] * 4,
        out_specs=VMEM,
        out_shape=jax.ShapeDtypeStruct((32, 16, 128), BF16),
        scratch_shapes=[pltpu.VMEM((128, 128), F32), pltpu.VMEM((512, 128), F32)],
        compiler_params=pltpu.CompilerParams(vmem_limit_bytes=4 << 20),
        name="gate",
    )(slot, gz, gy, *pieces)


S, D = (0, 1), (2, 3)


def to_previous(slots):
    even = [slots[4 + S[h]] - 0.25 * (slots[D[h]] + slots[4 + D[h]]) for h in range(2)]
    return slots[:4] + even


def to_next(slots):
    return [slots[4 + D[h]] for h in range(2)]


def project_kernel(gz_ref, gy_ref, parts_ref, proj_ref, own_ref, sent_ref, held, turned):
    chunks = []
    for k in range(8):
        chunk = parts_ref[4 * k].astype(F32)
        for i in range(1, 4):
            chunk = chunk + parts_ref[4 * k + i].astype(F32)
        chunks.append(chunk.astype(BF16))
    held[...] = jnp.dot(
        jnp.concatenate(chunks, axis=1), proj_ref[...], preferred_element_type=F32
    )
    block = lax.broadcasted_iota(jnp.int32, (4, 128), 1) // 32
    for b1 in range(4):
        rows = [held[i * 4 : (i + 1) * 4, b1 * 128 : (b1 + 1) * 128] for i in range(4)]
        hz1, hy1 = b1 // 2, b1 % 2
        for b2 in range(4):
            hz2, hy2 = b2 // 2, b2 % 2
            merged = None
            for i in range(4):
                shift = ((i - b2) % 4) * 32
                moved = rows[i] if shift == 0 else pltpu.roll(rows[i], shift, 1)
                merged = moved if merged is None else jnp.where(block == i, moved, merged)
            for z in range(2):
                for y in range(2):
                    row = merged[z * 2 + y : z * 2 + y + 1, :]
                    z_slot, y_slot = z * 4 + hz1 * 2 + hz2, y * 4 + hy1 * 2 + hy2
                    own_ref[z_slot, y_slot : y_slot + 1, :] = row
                    turned[y_slot, z_slot : z_slot + 1, :] = row

    gz, gy = gz_ref[0], gy_ref[0]
    sent_ref[...] = jnp.zeros_like(sent_ref)

    def send(dz, dy, slots):
        at = ((gz + dz) % 4) * 4 + (gy + dy) % 4
        for k in range(len(slots) // 2):
            sent_ref[at, k] = jnp.concatenate(slots[2 * k : 2 * k + 2], axis=0).astype(BF16)

    by_z = [own_ref[k] for k in range(8)]
    by_y = [turned[k] for k in range(8)]
    for dy in (3, 0, 1):
        send(3, dy, to_previous(by_z))
        send(1, dy, to_next(by_z))
    send(0, 3, to_previous(by_y))
    send(0, 1, to_next(by_y))


def project(gz, gy, parts, proj_weight):
    return pl.pallas_call(
        project_kernel,
        in_specs=[SMEM] * 2 + [VMEM] * 2,
        out_specs=[VMEM] * 2,
        out_shape=[
            jax.ShapeDtypeStruct((8, 8, 128), F32),
            jax.ShapeDtypeStruct((16, 3, 16, 128), BF16),
        ],
        scratch_shapes=[pltpu.VMEM((16, 512), F32), pltpu.VMEM((8, 8, 128), F32)],
        compiler_params=pltpu.CompilerParams(vmem_limit_bytes=8 << 20),
        name="project",
    )(gz, gy, parts, proj_weight)


def lift_pair(low, high):
    n = len(low)
    even = [low[i] - 0.25 * (high[i - 1] + high[i]) for i in range(1, n)]
    odd = [high[i] + 0.5 * (even[i - 1] + even[i]) for i in range(1, n - 1)]
    result = []
    for i in range(n - 2):
        result += [even[i], odd[i]]
    return result + [even[n - 2]]


def two_levels(before, own, after):
    middle = []
    for h in range(2):
        low = [own[S[h]], own[4 + S[h]], after[S[h]]]
        high = [before[h], own[D[h]], own[4 + D[h]], after[D[h]]]
        even = [low[i] - 0.25 * (high[i] + high[i + 1]) for i in range(3)] + [after[4 + h]]
        odd = [high[i + 1] + 0.5 * (even[i] + even[i + 1]) for i in range(3)]
        middle.append([odd[0], even[1], odd[1], even[2], odd[2], even[3]])
    return lift_pair(middle[0], middle[1])[:8]


def lift_kernel(gz_ref, gy_ref, own_ref, got_ref, out_ref, across, tall):
    gz, gy = gz_ref[0], gy_ref[0]
    at = lambda dz, dy: ((gz + dz) % 4) * 4 + (gy + dy) % 4
    after, before = at(0, 1), at(0, 3)

    def slots_from(source, count):
        for k in range(count // 2):
            pair = got_ref[source, k].astype(F32)
            yield pair[:8]
            yield pair[8:]

    for k, cells in enumerate(slots_from(after, 6)):
        across[1, :, k, :] = cells
    for k, cells in enumerate(slots_from(before, 2)):
        across[0, :, 6 + k, :] = cells
    sub = lax.broadcasted_iota(jnp.int32, (8, 128), 0)

    def shortened(cells):
        even = cells - 0.25 * (pltpu.roll(cells, 2, 0) + pltpu.roll(cells, 6, 0))
        return jnp.where(sub < 4, cells, even)

    for side, dy in ((0, 3), (1, 1), (2, 0)):
        change = shortened if side == 1 else lambda cells: cells
        below = [change(cells) for cells in slots_from(at(3, dy), 2)]
        above = [change(cells) for cells in slots_from(at(1, dy), 6)]
        centre = [own_ref[k] if side == 2 else across[side, k] for k in range(8)]
        for i, fine in enumerate(two_levels(below, centre, above)):
            tall[side, :, i, :] = fine
    fine = two_levels(
        [tall[0, 6 + k] for k in range(2)],
        [tall[2, k] for k in range(8)],
        [tall[1, k] for k in range(6)],
    )
    for i in range(8):
        out_ref[:, i, :] = fine[i]


def lift(gz, gy, own, got):
    return pl.pallas_call(
        lift_kernel,
        in_specs=[SMEM] * 2 + [VMEM] * 2,
        out_specs=VMEM,
        out_shape=jax.ShapeDtypeStruct((8, 8, 128), F32),
        scratch_shapes=[pltpu.VMEM((2, 8, 8, 128), F32), pltpu.VMEM((3, 8, 8, 128), F32)],
        compiler_params=pltpu.CompilerParams(vmem_limit_bytes=4 << 20),
        name="lift",
    )(gz, gy, own, got)


def on_device(volume, conv_weight, proj_weight):
    half = lax.axis_index("half")
    slot = ((lax.axis_index("ring") * 2 + half) % 4).reshape(1)
    gz, gy = (lax.axis_index(axis).reshape(1) for axis in ("gz", "gy"))
    own = lax.all_gather(volume.reshape(4, 32, 128), "ring", axis=0, tiled=False)
    other = lax.ppermute(own, "half", [(0, 1), (1, 0)])
    total, rest = own_half(half.reshape(1), own, conv_weight.reshape(3, 576, 1024))
    keep, to_y, to_z, to_corner = other_half(other, rest, total)
    step = [(i, (i + 1) % 4) for i in range(4)]
    both = [(a * 4 + b, c * 4 + d) for a, c in step for b, d in step]
    from_corner = lax.ppermute(to_corner, ("gz", "gy"), both)
    from_z = lax.ppermute(to_z, "gz", step)
    from_y = lax.ppermute(to_y, "gy", step)
    sent = gate(slot, gz, gy, keep, from_y, from_z, from_corner)
    parts = lax.all_to_all(sent, ("ring", "half"), split_axis=0, concat_axis=0, tiled=True)
    coefficients, messages = project(gz, gy, parts, proj_weight)
    got = lax.all_to_all(messages, ("gz", "gy"), split_axis=0, concat_axis=0, tiled=True)
    return lift(gz, gy, coefficients, got)


def solution(mesh):
    split = Mesh(mesh.devices.reshape(4, 4, 16, 2), ("gz", "gy", "ring", "half"))
    col = ("ring", "half")
    return jax.shard_map(
        on_device,
        mesh=split,
        in_specs=(P("gz", "gy", col, None), P(None, None, col, None), P()),
        out_specs=P("gz", "gy", col),
        check_vma=False,
    )
```

```python
import jax
import jax.numpy as jnp
from jax import lax
from jax.experimental import pallas as pl
from jax.experimental.pallas import tpu as pltpu
from jax.sharding import Mesh, PartitionSpec as P


F32 = jnp.float32
BF16 = jnp.bfloat16
VMEM = pl.BlockSpec(memory_space=pltpu.VMEM)
SMEM = pl.BlockSpec(memory_space=pltpu.SMEM)


ORDER = (0, 2, 1, 3)


def place_of(k):
    return 4 * (k // 4) + ORDER.index(k % 4)


def spread_terms(products, lane):
    for dy in range(3):
        for z in range(2):
            for y in range(2):
                row = z * 2 + y
                before, centre, after = (
                    products[(dy * 3 + dx) * 64 : (dy * 3 + dx + 1) * 64, row * 128 : (row + 1) * 128]
                    for dx in range(3)
                )
                yield z + 2, y + 2 - dy, (
                    centre
                    + jnp.where(lane == 0, 0.0, pltpu.roll(before, 1, 1))
                    + jnp.where(lane == 127, 0.0, pltpu.roll(after, 127, 1))
                )


def own_half_kernel(half_ref, own_ref, weight_ref, total_ref, rest_ref, cells, mine):
    step = pl.program_id(0)

    @pl.when(step == 0)
    def _():
        for k in range(16):
            for row in range(4):
                cells[place_of(k), :, row * 128 : (row + 1) * 128] = own_ref[k, row]
        total_ref[...] = jnp.zeros_like(total_ref)

    lane = lax.broadcasted_iota(jnp.int32, (64, 128), 1)
    first = half_ref[0] == 0
    for r in range(9):
        rows = slice(r * 64, (r + 1) * 64)
        for u in range(4):
            left = weight_ref[0, rows, u * 256 : u * 256 + 128].astype(F32)
            right = weight_ref[0, rows, u * 256 + 128 : (u + 1) * 256].astype(F32)
            keep = lane // 32 % 2 == 0
            even = jnp.where(keep, left, pltpu.roll(right, 32, 1)).astype(BF16)
            odd = jnp.where(keep, pltpu.roll(left, 96, 1), right).astype(BF16)
            mine[rows, u * 128 : (u + 1) * 128] = jnp.where(first, even, odd)
            rest_ref[0, rows, u * 128 : (u + 1) * 128] = jnp.where(first, odd, even)

    products = jnp.dot(mine[...], cells[...].reshape(512, 512), preferred_element_type=F32)
    for z, y, term in spread_terms(products, lane):
        total_ref[z - step, y] += term


def own_half(half, own, weight):
    return pl.pallas_call(
        own_half_kernel,
        grid=(3,),
        in_specs=[SMEM, VMEM, pl.BlockSpec((1, 576, 1024), lambda i: (i, 0, 0))],
        out_specs=[
            pl.BlockSpec((4, 4, 64, 128), lambda i: (0, 0, 0, 0)),
            pl.BlockSpec((1, 576, 512), lambda i: (i, 0, 0)),
        ],
        out_shape=[
            jax.ShapeDtypeStruct((4, 4, 64, 128), F32),
            jax.ShapeDtypeStruct((3, 576, 512), BF16),
        ],
        scratch_shapes=[pltpu.VMEM((16, 32, 512), BF16), pltpu.VMEM((576, 512), BF16)],
        compiler_params=pltpu.CompilerParams(vmem_limit_bytes=16 << 20),
        cost_estimate=pl.CostEstimate(flops=1 << 30, bytes_accessed=6 << 20, transcendentals=0),
        name="own_half",
    )(half, own, weight)


def other_half_kernel(other_ref, rest_ref, total_ref, keep_ref, y_ref, z_ref, corner_ref, cells):
    for k in range(16):
        for row in range(4):
            cells[place_of(k), :, row * 128 : (row + 1) * 128] = other_ref[k, row]
    sums = ((keep_ref, y_ref), (z_ref, corner_ref))
    for z in range(4):
        for y in range(4):
            sums[z // 2][y // 2][z % 2, y % 2] = total_ref[z, y]
    lane = lax.broadcasted_iota(jnp.int32, (64, 128), 1)
    for step in range(3):
        products = jnp.dot(rest_ref[step], cells[...].reshape(512, 512), preferred_element_type=F32)
        for z, y, term in spread_terms(products, lane):
            z = z - step
            sums[z // 2][y // 2][z % 2, y % 2] += term


def other_half(other, rest, total):
    return pl.pallas_call(
        other_half_kernel,
        in_specs=[VMEM] * 3,
        out_specs=[VMEM] * 4,
        out_shape=[jax.ShapeDtypeStruct((2, 2, 64, 128), F32)] * 4,
        scratch_shapes=[pltpu.VMEM((16, 32, 512), BF16)],
        compiler_params=pltpu.CompilerParams(vmem_limit_bytes=16 << 20),
        cost_estimate=pl.CostEstimate(flops=1 << 30, bytes_accessed=3 << 20, transcendentals=0),
        name="other_half",
    )(other, rest, total)


def gate_kernel(gz_ref, gy_ref, keep_ref, y_ref, z_ref, corner_ref, out_ref, turned):
    inside = [jnp.where(ref[0] > 0, 1.0, 0.0) for ref in (gz_ref, gy_ref)]
    pieces = []
    for z in range(2):
        for y in range(2):
            z_own, z_before = ((inside[0], 1.0), (1.0, inside[0]))[z]
            y_own, y_before = ((inside[1], 1.0), (1.0, inside[1]))[y]
            conv_out = (
                keep_ref[z, y] * (z_own * y_own)
                + y_ref[z, y] * (z_own * y_before)
                + z_ref[z, y] * (z_before * y_own)
                + corner_ref[z, y] * (z_before * y_before)
            )
            gate, value = conv_out[:32], conv_out[32:]
            pieces.append(gate / (1.0 + jnp.exp(-gate)) * value)
    turned[...] = jnp.concatenate(pieces, axis=0).T
    for k in range(32):
        out_ref[k] = turned[4 * k : 4 * k + 4, :].astype(BF16)


def gate(gz, gy, *pieces):
    return pl.pallas_call(
        gate_kernel,
        in_specs=[SMEM] * 2 + [VMEM] * 4,
        out_specs=VMEM,
        out_shape=jax.ShapeDtypeStruct((32, 4, 128), BF16),
        scratch_shapes=[pltpu.VMEM((128, 128), F32)],
        compiler_params=pltpu.CompilerParams(vmem_limit_bytes=4 << 20),
        name="gate",
    )(gz, gy, *pieces)


S, D = (0, 1), (2, 3)


def to_previous(slots):
    even = [slots[4 + S[h]] - 0.25 * (slots[D[h]] + slots[4 + D[h]]) for h in range(2)]
    return slots[:4] + even


def to_next(slots):
    return [slots[4 + D[h]] for h in range(2)]


def swapped_blocks(rows, block, place):
    merged = None
    for i in range(4):
        shift = ((i - place) % 4) * 32
        moved = rows[i] if shift == 0 else pltpu.roll(rows[i], shift, 1)
        merged = moved if merged is None else jnp.where(block == i, moved, merged)
    return merged


def project_kernel(gz_ref, gy_ref, parts_ref, proj_ref, own_ref, sent_ref, gathered, held, turned):
    block = lax.broadcasted_iota(jnp.int32, (4, 128), 1) // 32
    for k in range(8):
        rows = [parts_ref[4 * k + i].astype(F32) for i in range(4)]
        for cell in range(4):
            gathered[cell * 4 : cell * 4 + 4, k * 128 : (k + 1) * 128] = swapped_blocks(rows, block, cell)
    product = jnp.dot(gathered[...].astype(BF16), proj_ref[...], preferred_element_type=F32)
    for b1 in range(4):
        held[b1] = product[:, b1 * 128 : (b1 + 1) * 128]
    for b1 in range(4):
        rows = [held[b1, pl.ds(i, 4, stride=4), :] for i in range(4)]
        hz1, hy1 = b1 // 2, b1 % 2
        for b2 in range(4):
            hz2, hy2 = b2 // 2, b2 % 2
            merged = swapped_blocks(rows, block, b2)
            for z in range(2):
                for y in range(2):
                    row = merged[z * 2 + y : z * 2 + y + 1, :]
                    z_slot, y_slot = z * 4 + hz1 * 2 + hz2, y * 4 + hy1 * 2 + hy2
                    own_ref[z_slot, y_slot : y_slot + 1, :] = row
                    turned[y_slot, z_slot : z_slot + 1, :] = row

    gz, gy = gz_ref[0], gy_ref[0]
    sent_ref[...] = jnp.zeros_like(sent_ref)

    def send(dz, dy, slots):
        at = ((gz + dz) % 4) * 4 + (gy + dy) % 4
        for k in range(len(slots) // 2):
            sent_ref[at, k] = jnp.concatenate(slots[2 * k : 2 * k + 2], axis=0).astype(BF16)

    by_z = [own_ref[k] for k in range(8)]
    by_y = [turned[k] for k in range(8)]
    for dy in (3, 0, 1):
        send(3, dy, to_previous(by_z))
        send(1, dy, to_next(by_z))
    send(0, 3, to_previous(by_y))
    send(0, 1, to_next(by_y))


def project(gz, gy, parts, proj_weight):
    return pl.pallas_call(
        project_kernel,
        in_specs=[SMEM] * 2 + [VMEM] * 2,
        out_specs=[VMEM] * 2,
        out_shape=[
            jax.ShapeDtypeStruct((8, 8, 128), F32),
            jax.ShapeDtypeStruct((16, 3, 16, 128), BF16),
        ],
        scratch_shapes=[
            pltpu.VMEM((16, 1024), F32),
            pltpu.VMEM((4, 16, 128), F32),
            pltpu.VMEM((8, 8, 128), F32),
        ],
        compiler_params=pltpu.CompilerParams(vmem_limit_bytes=8 << 20),
        name="project",
    )(gz, gy, parts, proj_weight)


def lift_pair(low, high):
    n = len(low)
    even = [low[i] - 0.25 * (high[i - 1] + high[i]) for i in range(1, n)]
    odd = [high[i] + 0.5 * (even[i - 1] + even[i]) for i in range(1, n - 1)]
    result = []
    for i in range(n - 2):
        result += [even[i], odd[i]]
    return result + [even[n - 2]]


def two_levels(before, own, after):
    middle = []
    for h in range(2):
        low = [own[S[h]], own[4 + S[h]], after[S[h]]]
        high = [before[h], own[D[h]], own[4 + D[h]], after[D[h]]]
        even = [low[i] - 0.25 * (high[i] + high[i + 1]) for i in range(3)] + [after[4 + h]]
        odd = [high[i + 1] + 0.5 * (even[i] + even[i + 1]) for i in range(3)]
        middle.append([odd[0], even[1], odd[1], even[2], odd[2], even[3]])
    return lift_pair(middle[0], middle[1])[:8]


def lift_kernel(gz_ref, gy_ref, own_ref, got_ref, out_ref, across, tall):
    gz, gy = gz_ref[0], gy_ref[0]
    at = lambda dz, dy: ((gz + dz) % 4) * 4 + (gy + dy) % 4
    after, before = at(0, 1), at(0, 3)

    def slots_from(source, count):
        for k in range(count // 2):
            pair = got_ref[source, k].astype(F32)
            yield pair[:8]
            yield pair[8:]

    for k, cells in enumerate(slots_from(after, 6)):
        across[1, :, k, :] = cells
    for k, cells in enumerate(slots_from(before, 2)):
        across[0, :, 6 + k, :] = cells
    sub = lax.broadcasted_iota(jnp.int32, (8, 128), 0)

    def shortened(cells):
        even = cells - 0.25 * (pltpu.roll(cells, 2, 0) + pltpu.roll(cells, 6, 0))
        return jnp.where(sub < 4, cells, even)

    for side, dy in ((0, 3), (1, 1), (2, 0)):
        change = shortened if side == 1 else lambda cells: cells
        below = [change(cells) for cells in slots_from(at(3, dy), 2)]
        above = [change(cells) for cells in slots_from(at(1, dy), 6)]
        centre = [own_ref[k] if side == 2 else across[side, k] for k in range(8)]
        for i, fine in enumerate(two_levels(below, centre, above)):
            tall[side, :, i, :] = fine
    fine = two_levels(
        [tall[0, 6 + k] for k in range(2)],
        [tall[2, k] for k in range(8)],
        [tall[1, k] for k in range(6)],
    )
    for i in range(8):
        out_ref[:, i, :] = fine[i]


def lift(gz, gy, own, got):
    return pl.pallas_call(
        lift_kernel,
        in_specs=[SMEM] * 2 + [VMEM] * 2,
        out_specs=VMEM,
        out_shape=jax.ShapeDtypeStruct((8, 8, 128), F32),
        scratch_shapes=[pltpu.VMEM((2, 8, 8, 128), F32), pltpu.VMEM((3, 8, 8, 128), F32)],
        compiler_params=pltpu.CompilerParams(vmem_limit_bytes=4 << 20),
        name="lift",
    )(gz, gy, own, got)


def on_device(volume, conv_weight, proj_weight):
    half = lax.axis_index("half")
    gz, gy = (lax.axis_index(axis).reshape(1) for axis in ("gz", "gy"))
    own = lax.all_gather(volume.reshape(4, 32, 128), "ring", axis=0, tiled=False)
    other = lax.ppermute(own, "half", [(0, 1), (1, 0)])
    total, rest = own_half(half.reshape(1), own, conv_weight.reshape(3, 576, 1024))
    keep, to_y, to_z, to_corner = other_half(other, rest, total)
    step = [(i, (i + 1) % 4) for i in range(4)]
    both = [(a * 4 + b, c * 4 + d) for a, c in step for b, d in step]
    from_corner = lax.ppermute(to_corner, ("gz", "gy"), both)
    from_z = lax.ppermute(to_z, "gz", step)
    from_y = lax.ppermute(to_y, "gy", step)
    sent = gate(gz, gy, keep, from_y, from_z, from_corner)
    parts = lax.all_to_all(sent, ("ring", "half"), split_axis=0, concat_axis=0, tiled=True)
    coefficients, messages = project(gz, gy, parts, proj_weight)
    got = lax.all_to_all(messages, ("gz", "gy"), split_axis=0, concat_axis=0, tiled=True)
    return lift(gz, gy, coefficients, got)


def solution(mesh):
    split = Mesh(mesh.devices.reshape(4, 4, 16, 2), ("gz", "gy", "ring", "half"))
    col = ("ring", "half")
    return jax.shard_map(
        on_device,
        mesh=split,
        in_specs=(P("gz", "gy", col, None), P(None, None, col, None), P()),
        out_specs=P("gz", "gy", col),
        check_vma=False,
    )
```

```python
import jax
import jax.numpy as jnp
from jax import lax
from jax.experimental import pallas as pl
from jax.experimental.pallas import tpu as pltpu
from jax.sharding import Mesh, PartitionSpec as P


F32 = jnp.float32
BF16 = jnp.bfloat16
VMEM = pl.BlockSpec(memory_space=pltpu.VMEM)
SMEM = pl.BlockSpec(memory_space=pltpu.SMEM)


ORDER = (0, 2, 1, 3)


def place_of(k):
    return 4 * (k // 4) + ORDER.index(k % 4)


def spread_terms(products, lane):
    for dy in range(3):
        for z in range(2):
            for y in range(2):
                row = z * 2 + y
                before, centre, after = (
                    products[(dy * 3 + dx) * 64 : (dy * 3 + dx + 1) * 64, row * 128 : (row + 1) * 128]
                    for dx in range(3)
                )
                yield z + 2, y + 2 - dy, (
                    centre
                    + jnp.where(lane == 0, 0.0, pltpu.roll(before, 1, 1))
                    + jnp.where(lane == 127, 0.0, pltpu.roll(after, 127, 1))
                )


def own_half_kernel(half_ref, own_ref, weight_ref, total_ref, rest_ref, cells, mine):
    step = pl.program_id(0)

    @pl.when(step == 0)
    def _():
        for k in range(16):
            for row in range(4):
                cells[place_of(k), :, row * 128 : (row + 1) * 128] = own_ref[k, row]
        total_ref[...] = jnp.zeros_like(total_ref)

    lane = lax.broadcasted_iota(jnp.int32, (64, 128), 1)
    first = half_ref[0] == 0
    for r in range(9):
        rows = slice(r * 64, (r + 1) * 64)
        for u in range(4):
            left = weight_ref[0, rows, u * 256 : u * 256 + 128].astype(F32)
            right = weight_ref[0, rows, u * 256 + 128 : (u + 1) * 256].astype(F32)
            keep = lane // 32 % 2 == 0
            even = jnp.where(keep, left, pltpu.roll(right, 32, 1)).astype(BF16)
            odd = jnp.where(keep, pltpu.roll(left, 96, 1), right).astype(BF16)
            mine[rows, u * 128 : (u + 1) * 128] = jnp.where(first, even, odd)
            rest_ref[0, rows, u * 128 : (u + 1) * 128] = jnp.where(first, odd, even)

    products = jnp.dot(mine[...], cells[...].reshape(512, 512), preferred_element_type=F32)
    for z, y, term in spread_terms(products, lane):
        total_ref[z - step, y] += term


def own_half(half, own, weight):
    return pl.pallas_call(
        own_half_kernel,
        grid=(3,),
        in_specs=[SMEM, VMEM, pl.BlockSpec((1, 576, 1024), lambda i: (i, 0, 0))],
        out_specs=[
            pl.BlockSpec((4, 4, 64, 128), lambda i: (0, 0, 0, 0)),
            pl.BlockSpec((1, 576, 512), lambda i: (i, 0, 0)),
        ],
        out_shape=[
            jax.ShapeDtypeStruct((4, 4, 64, 128), F32),
            jax.ShapeDtypeStruct((3, 576, 512), BF16),
        ],
        scratch_shapes=[pltpu.VMEM((16, 32, 512), BF16), pltpu.VMEM((576, 512), BF16)],
        compiler_params=pltpu.CompilerParams(vmem_limit_bytes=16 << 20),
        cost_estimate=pl.CostEstimate(flops=1 << 30, bytes_accessed=6 << 20, transcendentals=0),
        name="own_half",
    )(half, own, weight)


def other_half_kernel(other_ref, rest_ref, total_ref, keep_ref, y_ref, z_ref, corner_ref, cells, sides):
    for k in range(16):
        for row in range(4):
            cells[place_of(k), :, row * 128 : (row + 1) * 128] = other_ref[k, row]
    sums = ((keep_ref, y_ref), (z_ref, corner_ref))
    for part in range(3):
        sides[part] = jnp.zeros_like(sides[part])
    for step in range(3):
        products = jnp.dot(rest_ref[step], cells[...].reshape(512, 512), preferred_element_type=F32)
        for dy in range(3):
            for z in range(2):
                for y in range(2):
                    row = z * 2 + y
                    for dx in range(3):
                        sides[dx, z + 2 - step, y + 2 - dy] += products[
                            (dy * 3 + dx) * 64 : (dy * 3 + dx + 1) * 64, row * 128 : (row + 1) * 128
                        ]
    lane = lax.broadcasted_iota(jnp.int32, (64, 128), 1)
    for z in range(4):
        for y in range(4):
            sums[z // 2][y // 2][z % 2, y % 2] = (
                total_ref[z, y]
                + sides[1, z, y]
                + jnp.where(lane == 0, 0.0, pltpu.roll(sides[0, z, y], 1, 1))
                + jnp.where(lane == 127, 0.0, pltpu.roll(sides[2, z, y], 127, 1))
            )


def other_half(other, rest, total):
    return pl.pallas_call(
        other_half_kernel,
        in_specs=[VMEM] * 3,
        out_specs=[VMEM] * 4,
        out_shape=[jax.ShapeDtypeStruct((2, 2, 64, 128), F32)] * 4,
        scratch_shapes=[pltpu.VMEM((16, 32, 512), BF16), pltpu.VMEM((3, 4, 4, 64, 128), F32)],
        compiler_params=pltpu.CompilerParams(vmem_limit_bytes=16 << 20),
        cost_estimate=pl.CostEstimate(flops=1 << 30, bytes_accessed=3 << 20, transcendentals=0),
        name="other_half",
    )(other, rest, total)


def gate_kernel(gz_ref, gy_ref, keep_ref, y_ref, z_ref, corner_ref, out_ref, turned):
    inside = [jnp.where(ref[0] > 0, 1.0, 0.0) for ref in (gz_ref, gy_ref)]
    pieces = []
    for z in range(2):
        for y in range(2):
            z_own, z_before = ((inside[0], 1.0), (1.0, inside[0]))[z]
            y_own, y_before = ((inside[1], 1.0), (1.0, inside[1]))[y]
            conv_out = (
                keep_ref[z, y] * (z_own * y_own)
                + y_ref[z, y] * (z_own * y_before)
                + z_ref[z, y] * (z_before * y_own)
                + corner_ref[z, y] * (z_before * y_before)
            )
            gate, value = conv_out[:32], conv_out[32:]
            pieces.append(gate / (1.0 + jnp.exp(-gate)) * value)
    turned[...] = jnp.concatenate(pieces, axis=0).T
    for k in range(32):
        out_ref[k] = turned[4 * k : 4 * k + 4, :].astype(BF16)


def gate(gz, gy, *pieces):
    return pl.pallas_call(
        gate_kernel,
        in_specs=[SMEM] * 2 + [VMEM] * 4,
        out_specs=VMEM,
        out_shape=jax.ShapeDtypeStruct((32, 4, 128), BF16),
        scratch_shapes=[pltpu.VMEM((128, 128), F32)],
        compiler_params=pltpu.CompilerParams(vmem_limit_bytes=4 << 20),
        name="gate",
    )(gz, gy, *pieces)


S, D = (0, 1), (2, 3)


def to_previous(slots):
    even = [slots[4 + S[h]] - 0.25 * (slots[D[h]] + slots[4 + D[h]]) for h in range(2)]
    return slots[:4] + even


def to_next(slots):
    return [slots[4 + D[h]] for h in range(2)]


def swapped_blocks(rows, block, place):
    merged = None
    for i in range(4):
        shift = ((i - place) % 4) * 32
        moved = rows[i] if shift == 0 else pltpu.roll(rows[i], shift, 1)
        merged = moved if merged is None else jnp.where(block == i, moved, merged)
    return merged


def project_kernel(gz_ref, gy_ref, parts_ref, proj_ref, own_ref, sent_ref, gathered, held, turned):
    block = lax.broadcasted_iota(jnp.int32, (4, 128), 1) // 32
    for k in range(8):
        rows = [parts_ref[4 * k + i].astype(F32) for i in range(4)]
        for cell in range(4):
            gathered[cell * 4 : cell * 4 + 4, k * 128 : (k + 1) * 128] = swapped_blocks(rows, block, cell)
    product = jnp.dot(gathered[...].astype(BF16), proj_ref[...], preferred_element_type=F32)
    for b1 in range(4):
        held[b1] = product[:, b1 * 128 : (b1 + 1) * 128]
    for b1 in range(4):
        rows = [held[b1, pl.ds(i, 4, stride=4), :] for i in range(4)]
        hz1, hy1 = b1 // 2, b1 % 2
        for b2 in range(4):
            hz2, hy2 = b2 // 2, b2 % 2
            merged = swapped_blocks(rows, block, b2)
            for z in range(2):
                for y in range(2):
                    row = merged[z * 2 + y : z * 2 + y + 1, :]
                    z_slot, y_slot = z * 4 + hz1 * 2 + hz2, y * 4 + hy1 * 2 + hy2
                    own_ref[z_slot, y_slot : y_slot + 1, :] = row
                    turned[y_slot, z_slot : z_slot + 1, :] = row

    gz, gy = gz_ref[0], gy_ref[0]
    sent_ref[...] = jnp.zeros_like(sent_ref)

    def send(dz, dy, slots):
        at = ((gz + dz) % 4) * 4 + (gy + dy) % 4
        for k in range(len(slots) // 2):
            sent_ref[at, k] = jnp.concatenate(slots[2 * k : 2 * k + 2], axis=0).astype(BF16)

    by_z = [own_ref[k] for k in range(8)]
    by_y = [turned[k] for k in range(8)]
    for dy in (3, 0, 1):
        send(3, dy, to_previous(by_z))
        send(1, dy, to_next(by_z))
    send(0, 3, to_previous(by_y))
    send(0, 1, to_next(by_y))


def project(gz, gy, parts, proj_weight):
    return pl.pallas_call(
        project_kernel,
        in_specs=[SMEM] * 2 + [VMEM] * 2,
        out_specs=[VMEM] * 2,
        out_shape=[
            jax.ShapeDtypeStruct((8, 8, 128), F32),
            jax.ShapeDtypeStruct((16, 3, 16, 128), BF16),
        ],
        scratch_shapes=[
            pltpu.VMEM((16, 1024), F32),
            pltpu.VMEM((4, 16, 128), F32),
            pltpu.VMEM((8, 8, 128), F32),
        ],
        compiler_params=pltpu.CompilerParams(vmem_limit_bytes=8 << 20),
        name="project",
    )(gz, gy, parts, proj_weight)


def lift_pair(low, high):
    n = len(low)
    even = [low[i] - 0.25 * (high[i - 1] + high[i]) for i in range(1, n)]
    odd = [high[i] + 0.5 * (even[i - 1] + even[i]) for i in range(1, n - 1)]
    result = []
    for i in range(n - 2):
        result += [even[i], odd[i]]
    return result + [even[n - 2]]


def two_levels(before, own, after):
    middle = []
    for h in range(2):
        low = [own[S[h]], own[4 + S[h]], after[S[h]]]
        high = [before[h], own[D[h]], own[4 + D[h]], after[D[h]]]
        even = [low[i] - 0.25 * (high[i] + high[i + 1]) for i in range(3)] + [after[4 + h]]
        odd = [high[i + 1] + 0.5 * (even[i] + even[i + 1]) for i in range(3)]
        middle.append([odd[0], even[1], odd[1], even[2], odd[2], even[3]])
    return lift_pair(middle[0], middle[1])[:8]


def lift_kernel(gz_ref, gy_ref, own_ref, got_ref, out_ref, across, tall):
    gz, gy = gz_ref[0], gy_ref[0]
    at = lambda dz, dy: ((gz + dz) % 4) * 4 + (gy + dy) % 4
    after, before = at(0, 1), at(0, 3)

    def slots_from(source, count):
        for k in range(count // 2):
            pair = got_ref[source, k].astype(F32)
            yield pair[:8]
            yield pair[8:]

    for k, cells in enumerate(slots_from(after, 6)):
        across[1, :, k, :] = cells
    for k, cells in enumerate(slots_from(before, 2)):
        across[0, :, 6 + k, :] = cells
    sub = lax.broadcasted_iota(jnp.int32, (8, 128), 0)

    def shortened(cells):
        even = cells - 0.25 * (pltpu.roll(cells, 2, 0) + pltpu.roll(cells, 6, 0))
        return jnp.where(sub < 4, cells, even)

    for side, dy in ((0, 3), (1, 1), (2, 0)):
        change = shortened if side == 1 else lambda cells: cells
        below = [change(cells) for cells in slots_from(at(3, dy), 2)]
        above = [change(cells) for cells in slots_from(at(1, dy), 6)]
        centre = [own_ref[k] if side == 2 else across[side, k] for k in range(8)]
        for i, fine in enumerate(two_levels(below, centre, above)):
            tall[side, :, i, :] = fine
    fine = two_levels(
        [tall[0, 6 + k] for k in range(2)],
        [tall[2, k] for k in range(8)],
        [tall[1, k] for k in range(6)],
    )
    for i in range(8):
        out_ref[:, i, :] = fine[i]


def lift(gz, gy, own, got):
    return pl.pallas_call(
        lift_kernel,
        in_specs=[SMEM] * 2 + [VMEM] * 2,
        out_specs=VMEM,
        out_shape=jax.ShapeDtypeStruct((8, 8, 128), F32),
        scratch_shapes=[pltpu.VMEM((2, 8, 8, 128), F32), pltpu.VMEM((3, 8, 8, 128), F32)],
        compiler_params=pltpu.CompilerParams(vmem_limit_bytes=4 << 20),
        name="lift",
    )(gz, gy, own, got)


def on_device(volume, conv_weight, proj_weight):
    half = lax.axis_index("half")
    gz, gy = (lax.axis_index(axis).reshape(1) for axis in ("gz", "gy"))
    own = lax.all_gather(volume.reshape(128, 128), "ring", axis=0, tiled=True).reshape(16, 4, 32, 128)
    other = lax.ppermute(own, "half", [(0, 1), (1, 0)])
    total, rest = own_half(half.reshape(1), own, conv_weight.reshape(3, 576, 1024))
    keep, to_y, to_z, to_corner = other_half(other, rest, total)
    step = [(i, (i + 1) % 4) for i in range(4)]
    both = [(a * 4 + b, c * 4 + d) for a, c in step for b, d in step]
    from_corner = lax.ppermute(to_corner, ("gz", "gy"), both)
    from_z = lax.ppermute(to_z, "gz", step)
    from_y = lax.ppermute(to_y, "gy", step)
    sent = gate(gz, gy, keep, from_y, from_z, from_corner)
    parts = lax.all_to_all(sent, ("ring", "half"), split_axis=0, concat_axis=0, tiled=True)
    coefficients, messages = project(gz, gy, parts, proj_weight)
    got = lax.all_to_all(messages, ("gz", "gy"), split_axis=0, concat_axis=0, tiled=True)
    return lift(gz, gy, coefficients, got)


def solution(mesh):
    split = Mesh(mesh.devices.reshape(4, 4, 16, 2), ("gz", "gy", "ring", "half"))
    col = ("ring", "half")
    return jax.shard_map(
        on_device,
        mesh=split,
        in_specs=(P("gz", "gy", col, None), P(None, None, col, None), P()),
        out_specs=P("gz", "gy", col),
        check_vma=False,
    )
```

```python
import jax
import jax.numpy as jnp
from jax import lax
from jax.experimental import pallas as pl
from jax.experimental.pallas import tpu as pltpu
from jax.sharding import Mesh, PartitionSpec as P


F32 = jnp.float32
BF16 = jnp.bfloat16
VMEM = pl.BlockSpec(memory_space=pltpu.VMEM)
SMEM = pl.BlockSpec(memory_space=pltpu.SMEM)


ORDER = (0, 2, 1, 3)


def place_of(k):
    return 4 * (k // 4) + ORDER.index(k % 4)


def spread_terms(products, lane):
    for dy in range(3):
        for z in range(2):
            for y in range(2):
                row = z * 2 + y
                before, centre, after = (
                    products[(dy * 3 + dx) * 64 : (dy * 3 + dx + 1) * 64, row * 128 : (row + 1) * 128]
                    for dx in range(3)
                )
                yield z + 2, y + 2 - dy, (
                    centre
                    + jnp.where(lane == 0, 0.0, pltpu.roll(before, 1, 1))
                    + jnp.where(lane == 127, 0.0, pltpu.roll(after, 127, 1))
                )


def own_half_kernel(half_ref, own_ref, weight_ref, total_ref, rest_ref, cells, mine):
    step = pl.program_id(0)

    @pl.when(step == 0)
    def _():
        for k in range(16):
            for row in range(4):
                cells[place_of(k), :, row * 128 : (row + 1) * 128] = own_ref[k, row]
        total_ref[...] = jnp.zeros_like(total_ref)

    lane = lax.broadcasted_iota(jnp.int32, (64, 128), 1)
    first = half_ref[0] == 0
    for r in range(9):
        rows = slice(r * 64, (r + 1) * 64)
        for u in range(4):
            left = weight_ref[0, rows, u * 256 : u * 256 + 128].astype(F32)
            right = weight_ref[0, rows, u * 256 + 128 : (u + 1) * 256].astype(F32)
            keep = lane // 32 % 2 == 0
            even = jnp.where(keep, left, pltpu.roll(right, 32, 1)).astype(BF16)
            odd = jnp.where(keep, pltpu.roll(left, 96, 1), right).astype(BF16)
            mine[rows, u * 128 : (u + 1) * 128] = jnp.where(first, even, odd)
            rest_ref[0, rows, u * 128 : (u + 1) * 128] = jnp.where(first, odd, even)

    products = jnp.dot(mine[...], cells[...].reshape(512, 512), preferred_element_type=F32)
    for z, y, term in spread_terms(products, lane):
        total_ref[z - step, y] += term


def own_half(half, own, weight):
    return pl.pallas_call(
        own_half_kernel,
        grid=(3,),
        in_specs=[SMEM, VMEM, pl.BlockSpec((1, 576, 1024), lambda i: (i, 0, 0))],
        out_specs=[
            pl.BlockSpec((4, 4, 64, 128), lambda i: (0, 0, 0, 0)),
            pl.BlockSpec((1, 576, 512), lambda i: (i, 0, 0)),
        ],
        out_shape=[
            jax.ShapeDtypeStruct((4, 4, 64, 128), F32),
            jax.ShapeDtypeStruct((3, 576, 512), BF16),
        ],
        scratch_shapes=[pltpu.VMEM((16, 32, 512), BF16), pltpu.VMEM((576, 512), BF16)],
        compiler_params=pltpu.CompilerParams(vmem_limit_bytes=16 << 20),
        cost_estimate=pl.CostEstimate(flops=1 << 30, bytes_accessed=6 << 20, transcendentals=0),
        name="own_half",
    )(half, own, weight)


def add_products(products, step, first_dy, rows, sides, wanted):
    for at, dy in enumerate(range(first_dy, first_dy + products.shape[0] // 192)):
        for i, row in enumerate(rows):
            z, y = row // 2 + 2 - step, row % 2 + 2 - dy
            if wanted(z, y):
                for dx in range(3):
                    sides[dx, z, y] += products[
                        (at * 3 + dx) * 64 : (at * 3 + dx + 1) * 64, i * 128 : (i + 1) * 128
                    ]


def summed(total_ref, sides, z, y):
    lane = lax.broadcasted_iota(jnp.int32, (64, 128), 1)
    return (
        total_ref[z, y]
        + sides[1, z, y]
        + jnp.where(lane == 0, 0.0, pltpu.roll(sides[0, z, y], 1, 1))
        + jnp.where(lane == 127, 0.0, pltpu.roll(sides[2, z, y], 127, 1))
    )


def other_half_kernel(other_ref, rest_ref, total_ref, cells, y_ref, z_ref, corner_ref, sides):
    for k in range(16):
        for row in range(4):
            cells[place_of(k), :, row * 128 : (row + 1) * 128] = other_ref[k, row]
    sides[...] = jnp.zeros_like(sides)
    for step in range(3):
        count = 384 if step == 2 else 576
        products = jnp.dot(
            rest_ref[step, :count], cells[...].reshape(512, 512), preferred_element_type=F32
        )
        add_products(products, step, 0, range(4), sides, lambda z, y: z > 1 or y > 1)
    for ref, top, left in ((y_ref, 0, 2), (z_ref, 2, 0), (corner_ref, 2, 2)):
        for z in range(2):
            for y in range(2):
                ref[z, y] = summed(total_ref, sides, top + z, left + y)


def kept_kernel(cells, rest_ref, total_ref, keep_ref, sides):
    sides[...] = jnp.zeros_like(sides)
    for step, rows in ((1, (0, 1)), (2, (0, 1, 2, 3))):
        products = jnp.dot(
            rest_ref[step, 192:],
            cells[:, :, : len(rows) * 128].reshape(512, len(rows) * 128),
            preferred_element_type=F32,
        )
        add_products(products, step, 1, rows, sides, lambda z, y: z < 2 and y < 2)
    for z in range(2):
        for y in range(2):
            keep_ref[z, y] = summed(total_ref, sides, z, y)


def other_half(other, rest, total):
    piece = jax.ShapeDtypeStruct((2, 2, 64, 128), F32)
    params = pltpu.CompilerParams(vmem_limit_bytes=16 << 20)
    cells, to_y, to_z, to_corner = pl.pallas_call(
        other_half_kernel,
        in_specs=[VMEM] * 3,
        out_specs=[VMEM] * 4,
        out_shape=[jax.ShapeDtypeStruct((16, 32, 512), BF16), piece, piece, piece],
        scratch_shapes=[pltpu.VMEM((3, 4, 4, 64, 128), F32)],
        compiler_params=params,
        cost_estimate=pl.CostEstimate(flops=1 << 30, bytes_accessed=3 << 20, transcendentals=0),
        name="other_half",
    )(other, rest, total)
    keep = pl.pallas_call(
        kept_kernel,
        in_specs=[VMEM] * 3,
        out_specs=VMEM,
        out_shape=piece,
        scratch_shapes=[pltpu.VMEM((3, 2, 2, 64, 128), F32)],
        compiler_params=params,
        cost_estimate=pl.CostEstimate(flops=1 << 29, bytes_accessed=2 << 20, transcendentals=0),
        name="kept",
    )(cells, rest, total)
    return keep, to_y, to_z, to_corner


def gate_kernel(gz_ref, gy_ref, keep_ref, y_ref, z_ref, corner_ref, out_ref, turned):
    inside = [jnp.where(ref[0] > 0, 1.0, 0.0) for ref in (gz_ref, gy_ref)]
    pieces = []
    for z in range(2):
        for y in range(2):
            z_own, z_before = ((inside[0], 1.0), (1.0, inside[0]))[z]
            y_own, y_before = ((inside[1], 1.0), (1.0, inside[1]))[y]
            conv_out = (
                keep_ref[z, y] * (z_own * y_own)
                + y_ref[z, y] * (z_own * y_before)
                + z_ref[z, y] * (z_before * y_own)
                + corner_ref[z, y] * (z_before * y_before)
            )
            gate, value = conv_out[:32], conv_out[32:]
            pieces.append(gate / (1.0 + jnp.exp(-gate)) * value)
    turned[...] = jnp.concatenate(pieces, axis=0).T
    for k in range(32):
        out_ref[k] = turned[4 * k : 4 * k + 4, :].astype(BF16)


def gate(gz, gy, *pieces):
    return pl.pallas_call(
        gate_kernel,
        in_specs=[SMEM] * 2 + [VMEM] * 4,
        out_specs=VMEM,
        out_shape=jax.ShapeDtypeStruct((32, 4, 128), BF16),
        scratch_shapes=[pltpu.VMEM((128, 128), F32)],
        compiler_params=pltpu.CompilerParams(vmem_limit_bytes=4 << 20),
        name="gate",
    )(gz, gy, *pieces)


S, D = (0, 1), (2, 3)


def to_previous(slots):
    even = [slots[4 + S[h]] - 0.25 * (slots[D[h]] + slots[4 + D[h]]) for h in range(2)]
    return slots[:4] + even


def to_next(slots):
    return [slots[4 + D[h]] for h in range(2)]


def swapped_blocks(rows, block, place):
    merged = None
    for i in range(4):
        shift = ((i - place) % 4) * 32
        moved = rows[i] if shift == 0 else pltpu.roll(rows[i], shift, 1)
        merged = moved if merged is None else jnp.where(block == i, moved, merged)
    return merged


def project_kernel(gz_ref, gy_ref, parts_ref, proj_ref, own_ref, sent_ref, gathered, held, turned):
    block = lax.broadcasted_iota(jnp.int32, (4, 128), 1) // 32
    for k in range(8):
        rows = [parts_ref[4 * k + i].astype(F32) for i in range(4)]
        for cell in range(4):
            gathered[cell * 4 : cell * 4 + 4, k * 128 : (k + 1) * 128] = swapped_blocks(rows, block, cell)
    product = jnp.dot(gathered[...].astype(BF16), proj_ref[...], preferred_element_type=F32)
    for b1 in range(4):
        held[b1] = product[:, b1 * 128 : (b1 + 1) * 128]
    for b1 in range(4):
        rows = [held[b1, pl.ds(i, 4, stride=4), :] for i in range(4)]
        hz1, hy1 = b1 // 2, b1 % 2
        for b2 in range(4):
            hz2, hy2 = b2 // 2, b2 % 2
            merged = swapped_blocks(rows, block, b2)
            for z in range(2):
                for y in range(2):
                    row = merged[z * 2 + y : z * 2 + y + 1, :]
                    z_slot, y_slot = z * 4 + hz1 * 2 + hz2, y * 4 + hy1 * 2 + hy2
                    own_ref[z_slot, y_slot : y_slot + 1, :] = row
                    turned[y_slot, z_slot : z_slot + 1, :] = row

    gz, gy = gz_ref[0], gy_ref[0]
    sent_ref[...] = jnp.zeros_like(sent_ref)

    def send(dz, dy, slots):
        at = ((gz + dz) % 4) * 4 + (gy + dy) % 4
        for k in range(len(slots) // 2):
            sent_ref[at, k] = jnp.concatenate(slots[2 * k : 2 * k + 2], axis=0).astype(BF16)

    by_z = [own_ref[k] for k in range(8)]
    by_y = [turned[k] for k in range(8)]
    for dy in (3, 0, 1):
        send(3, dy, to_previous(by_z))
        send(1, dy, to_next(by_z))
    send(0, 3, to_previous(by_y))
    send(0, 1, to_next(by_y))


def project(gz, gy, parts, proj_weight):
    return pl.pallas_call(
        project_kernel,
        in_specs=[SMEM] * 2 + [VMEM] * 2,
        out_specs=[VMEM] * 2,
        out_shape=[
            jax.ShapeDtypeStruct((8, 8, 128), F32),
            jax.ShapeDtypeStruct((16, 3, 16, 128), BF16),
        ],
        scratch_shapes=[
            pltpu.VMEM((16, 1024), F32),
            pltpu.VMEM((4, 16, 128), F32),
            pltpu.VMEM((8, 8, 128), F32),
        ],
        compiler_params=pltpu.CompilerParams(vmem_limit_bytes=8 << 20),
        name="project",
    )(gz, gy, parts, proj_weight)


def lift_pair(low, high):
    n = len(low)
    even = [low[i] - 0.25 * (high[i - 1] + high[i]) for i in range(1, n)]
    odd = [high[i] + 0.5 * (even[i - 1] + even[i]) for i in range(1, n - 1)]
    result = []
    for i in range(n - 2):
        result += [even[i], odd[i]]
    return result + [even[n - 2]]


def two_levels(before, own, after):
    middle = []
    for h in range(2):
        low = [own[S[h]], own[4 + S[h]], after[S[h]]]
        high = [before[h], own[D[h]], own[4 + D[h]], after[D[h]]]
        even = [low[i] - 0.25 * (high[i] + high[i + 1]) for i in range(3)] + [after[4 + h]]
        odd = [high[i + 1] + 0.5 * (even[i] + even[i + 1]) for i in range(3)]
        middle.append([odd[0], even[1], odd[1], even[2], odd[2], even[3]])
    return lift_pair(middle[0], middle[1])[:8]


def lift_kernel(gz_ref, gy_ref, own_ref, got_ref, out_ref, across, tall):
    gz, gy = gz_ref[0], gy_ref[0]
    at = lambda dz, dy: ((gz + dz) % 4) * 4 + (gy + dy) % 4
    after, before = at(0, 1), at(0, 3)

    def slots_from(source, count):
        for k in range(count // 2):
            pair = got_ref[source, k].astype(F32)
            yield pair[:8]
            yield pair[8:]

    for k, cells in enumerate(slots_from(after, 6)):
        across[1, :, k, :] = cells
    for k, cells in enumerate(slots_from(before, 2)):
        across[0, :, 6 + k, :] = cells
    sub = lax.broadcasted_iota(jnp.int32, (8, 128), 0)

    def shortened(cells):
        even = cells - 0.25 * (pltpu.roll(cells, 2, 0) + pltpu.roll(cells, 6, 0))
        return jnp.where(sub < 4, cells, even)

    for side, dy in ((0, 3), (1, 1), (2, 0)):
        change = shortened if side == 1 else lambda cells: cells
        below = [change(cells) for cells in slots_from(at(3, dy), 2)]
        above = [change(cells) for cells in slots_from(at(1, dy), 6)]
        centre = [own_ref[k] if side == 2 else across[side, k] for k in range(8)]
        for i, fine in enumerate(two_levels(below, centre, above)):
            tall[side, :, i, :] = fine
    fine = two_levels(
        [tall[0, 6 + k] for k in range(2)],
        [tall[2, k] for k in range(8)],
        [tall[1, k] for k in range(6)],
    )
    for i in range(8):
        out_ref[:, i, :] = fine[i]


def lift(gz, gy, own, got):
    return pl.pallas_call(
        lift_kernel,
        in_specs=[SMEM] * 2 + [VMEM] * 2,
        out_specs=VMEM,
        out_shape=jax.ShapeDtypeStruct((8, 8, 128), F32),
        scratch_shapes=[pltpu.VMEM((2, 8, 8, 128), F32), pltpu.VMEM((3, 8, 8, 128), F32)],
        compiler_params=pltpu.CompilerParams(vmem_limit_bytes=4 << 20),
        name="lift",
    )(gz, gy, own, got)


def on_device(volume, conv_weight, proj_weight):
    half = lax.axis_index("half")
    gz, gy = (lax.axis_index(axis).reshape(1) for axis in ("gz", "gy"))
    own = lax.all_gather(volume.reshape(128, 128), "ring", axis=0, tiled=True).reshape(16, 4, 32, 128)
    other = lax.ppermute(own, "half", [(0, 1), (1, 0)])
    total, rest = own_half(half.reshape(1), own, conv_weight.reshape(3, 576, 1024))
    keep, to_y, to_z, to_corner = other_half(other, rest, total)
    step = [(i, (i + 1) % 4) for i in range(4)]
    both = [(a * 4 + b, c * 4 + d) for a, c in step for b, d in step]
    from_corner = lax.ppermute(to_corner, ("gz", "gy"), both)
    from_z = lax.ppermute(to_z, "gz", step)
    from_y = lax.ppermute(to_y, "gy", step)
    sent = gate(gz, gy, keep, from_y, from_z, from_corner)
    parts = lax.all_to_all(sent, ("ring", "half"), split_axis=0, concat_axis=0, tiled=True)
    coefficients, messages = project(gz, gy, parts, proj_weight)
    got = lax.all_to_all(messages, ("gz", "gy"), split_axis=0, concat_axis=0, tiled=True)
    return lift(gz, gy, coefficients, got)


def solution(mesh):
    split = Mesh(mesh.devices.reshape(4, 4, 16, 2), ("gz", "gy", "ring", "half"))
    col = ("ring", "half")
    return jax.shard_map(
        on_device,
        mesh=split,
        in_specs=(P("gz", "gy", col, None), P(None, None, col, None), P()),
        out_specs=P("gz", "gy", col),
        check_vma=False,
    )
```
